512 devices in a mesh: subtree: 32 (over x, y), front: 16 (over z, core).
Axes of the slice: x: 4, y: 8, z: 8, core: 2. Of those that a mesh axis runs over, the one named last changes fastest.
Arguments:
- modes_root: bfloat16 [1, 64, 12288], P(None, None, 'subtree'), may hold values from -6 to 6
- modes_mid: bfloat16 [2, 64, 8192], P(None, None, 'subtree'), may hold values from -6 to 6
- modes_low: bfloat16 [4, 64, 8192], P(None, None, 'subtree'), may hold values from -6 to 6
- factor_root: bfloat16 [1, 12288, 12288], P(None, 'front', 'subtree')
- factor_mid: bfloat16 [2, 8192, 8192], P(None, 'front', 'subtree')
- factor_low: bfloat16 [4, 8192, 8192], P(None, 'front', 'subtree')
- update_mid: bfloat16 [2, 4096, 8192], P(None, 'subtree', 'front'), may hold values from -0.0625 to 0.0625
- update_low: bfloat16 [4, 4096, 8192], P(None, 'subtree', 'front'), may hold values from -0.0625 to 0.0625
- map_mid: int32 [2, 32], P(None, 'subtree'), may hold values from 0 to 467, as said below
- map_low: int32 [4, 32], P(None, 'subtree'), may hold values from 0 to 471, as said below
- mass_vals: bfloat16 [480, 16, 128, 128], P('subtree', 'front'), may hold values from -0.125 to 0.125
- mass_cols: int32 [480, 16], P('subtree', 'front'), may hold values from 0 to 479, as said below
Outputs:
- solved_root: float32 [1, 64, 12288], P(None, None, 'subtree')
- solved_mid: float32 [2, 64, 8192], P(None, None, 'subtree')
- solved_low: float32 [4, 64, 8192], P(None, None, 'subtree')
- gram_stiff: float32 [64, 64], replicated
- gram_mass: float32 [64, 64], replicated
The draws below stay inside these ranges and needn't reach their ends.
Inputs may be any that keep to these rules, and one draw needn't show every extreme that they name: Rows of map_mid: each node has exactly one update block per owner: entry c of node n names a block (owner-major numbering) of the root separator's slice of owner c. Rows of map_low: each node has exactly one update block per owner: entry c of node n names a block of owner c in that owner's slice of the root separator or of middle node n // 2. `mass_cols`: entry 0 of block row r is r itself; every entry names a block of the same owner as r or of the owner just before or after it.
All inputs are finite; a program needn't handle non-finite values.
Results may differ from the reference program's by a relative error of at most 0.035.
Values may be sent and summed in bfloat16 or wider, within the bound.
No kernel may reach another device: no remote copies, remote signals or barrier semaphores. Data moves between devices by JAX's collectives and lax.ppermute only.
A program may use at most 64 MiB of HBM per device.

```python
import jax
import jax.numpy as jnp
from jax import lax

SEP_ROOT = 12288
SEP_MID = 8192
SEP_LOW = 8192
MODES = 64
UPDATE = 4096
BLOCK = 128
MASS_NNZ = 16
OWNERS = 32
LOCAL_BLOCKS = 15
ALL_BLOCKS = 480


def factor_draw(key, node_count, row_count):
    first_key, second_key = jax.random.split(key)
    lower_part = jax.random.normal(first_key, (node_count, row_count, row_count), jnp.float32)
    diagonal_vals = jax.random.uniform(second_key, (node_count, row_count), jnp.float32, 0.7, 1.3)
    row_index = lax.broadcasted_iota(jnp.int32, (row_count, row_count), 0)
    col_index = lax.broadcasted_iota(jnp.int32, (row_count, row_count), 1)
    below_mask = (col_index < row_index).astype(jnp.float32)
    unit_mask = (col_index == row_index).astype(jnp.float32)
    return lower_part * below_mask * row_count ** (-0.5) + diagonal_vals[:, :, None] * unit_mask


def draw_factor_root(key, part):
    return factor_draw(key, 1, SEP_ROOT).astype(jnp.bfloat16)


def draw_factor_mid(key, part):
    return factor_draw(key, 2, SEP_MID).astype(jnp.bfloat16)


def draw_factor_low(key, part):
    return factor_draw(key, 4, SEP_LOW).astype(jnp.bfloat16)


def distinct_pick(key, node_count, candidates):
    per_owner = UPDATE // BLOCK // OWNERS
    shape = (node_count, OWNERS, candidates)
    scores = jax.random.randint(key, shape, 0, 2 ** 20) * candidates + lax.broadcasted_iota(jnp.int32, shape, 2)
    chosen = jnp.argsort(scores, axis=2, stable=True)[:, :, :per_owner]
    return chosen.astype(jnp.int32)


def draw_map_mid(key, part):
    per_owner = UPDATE // BLOCK // OWNERS
    root_blocks = SEP_ROOT // BLOCK // OWNERS
    chosen = distinct_pick(key, 2, root_blocks)
    owner_base = lax.broadcasted_iota(jnp.int32, (2, OWNERS, per_owner), 1) * LOCAL_BLOCKS
    return (owner_base + chosen).reshape(2, OWNERS * per_owner)


def draw_map_low(key, part):
    per_owner = UPDATE // BLOCK // OWNERS
    root_blocks = SEP_ROOT // BLOCK // OWNERS
    mid_blocks = SEP_MID // BLOCK // OWNERS
    chosen = distinct_pick(key, 4, root_blocks + mid_blocks)
    parent = lax.broadcasted_iota(jnp.int32, (4, OWNERS, per_owner), 0) // 2
    local_block = jnp.where(chosen < root_blocks, chosen, root_blocks + parent * mid_blocks + (chosen - root_blocks))
    owner_base = lax.broadcasted_iota(jnp.int32, (4, OWNERS, per_owner), 1) * LOCAL_BLOCKS
    return (owner_base + local_block).reshape(4, OWNERS * per_owner)


def draw_mass_cols(key, part):
    shape = (ALL_BLOCKS, MASS_NNZ)
    row_block = lax.broadcasted_iota(jnp.int32, shape, 0)
    entry_index = lax.broadcasted_iota(jnp.int32, shape, 1)
    owner_of = row_block // LOCAL_BLOCKS
    low_end = jnp.maximum(owner_of - 1, 0) * LOCAL_BLOCKS
    high_end = jnp.minimum(owner_of + 2, OWNERS) * LOCAL_BLOCKS
    raw_values = jax.random.randint(key, shape, 0, 2 ** 20)
    picked = low_end + raw_values % (high_end - low_end)
    return jnp.where(entry_index == 0, row_block, picked)


def steps_of(stream_key, shape, shards, low, largest):
    level, own = 1.0, jax.random.fold_in(stream_key, 6)
    for axis_at, shards_of in shards:
        heights = jnp.exp(jax.random.uniform(jax.random.fold_in(own, axis_at), (shards_of,), jnp.float32, low / len(shards), largest / len(shards)))
        level = level * jnp.repeat(heights, shape[axis_at] // shards_of).reshape([-1 if axis == axis_at else 1 for axis in range(len(shape))])
    return level


def normal_values(own_key, shape, scale, limit, cuts=(), kind=jnp.bfloat16):
    loudness = steps_of(own_key, shape, cuts, -0.22, 0.18) if cuts else 1.0
    entries = jax.random.normal(own_key, shape, jnp.float32) * scale * loudness
    return jnp.minimum(jnp.maximum(entries, -limit), limit).astype(kind)


def setup_inputs(seed: int = 0) -> dict:
    key_of = jax.random.split(jax.random.key(seed), 13)
    modes_root = normal_values(key_of[0], (1, MODES, SEP_ROOT), 1.0, 6.0, ((2, 32),))
    modes_mid = normal_values(key_of[1], (2, MODES, SEP_MID), 1.0, 6.0, ((2, 32),))
    modes_low = normal_values(key_of[2], (4, MODES, SEP_LOW), 1.0, 6.0, ((2, 32),))
    factor_root = draw_factor_root(jax.random.fold_in(key_of[12], 71), 0)
    factor_mid = draw_factor_mid(jax.random.fold_in(key_of[12], 71), 0)
    factor_low = draw_factor_low(jax.random.fold_in(key_of[12], 71), 0)
    update_mid = normal_values(key_of[6], (2, UPDATE, SEP_MID), SEP_MID ** -0.5, 0.0625, ((1, 32), (2, 16)))
    update_low = normal_values(key_of[7], (4, UPDATE, SEP_LOW), SEP_LOW ** -0.5, 0.0625, ((1, 32), (2, 16)))
    map_mid = draw_map_mid(jax.random.fold_in(key_of[12], 71), 0)
    map_low = draw_map_low(jax.random.fold_in(key_of[12], 71), 0)
    mass_vals = normal_values(key_of[10], (ALL_BLOCKS, MASS_NNZ, BLOCK, BLOCK), (BLOCK * MASS_NNZ) ** -0.5, 0.125, ((0, 32), (1, 16)))
    mass_cols = draw_mass_cols(jax.random.fold_in(key_of[12], 71), 0)
    return dict(modes_root=modes_root, modes_mid=modes_mid, modes_low=modes_low, factor_root=factor_root, factor_mid=factor_mid, factor_low=factor_low, update_mid=update_mid, update_low=update_low, map_mid=map_mid, map_low=map_low, mass_vals=mass_vals, mass_cols=mass_cols)


def owner_order(levels):
    pieces = []
    for level_rows in levels:
        node_count, count_modes, row_count = level_rows.shape
        divided = level_rows.reshape(node_count, count_modes, OWNERS, row_count // OWNERS)
        pieces.append(jnp.transpose(divided, (1, 2, 0, 3)).reshape(count_modes, OWNERS, node_count * (row_count // OWNERS)))
    joined = jnp.concatenate(pieces, axis=2)
    return joined.reshape(joined.shape[0], -1)


def level_order(flat_rows, shapes):
    count_modes = flat_rows.shape[0]
    owner_grid = flat_rows.reshape(count_modes, OWNERS, -1)
    result = []
    offset = 0
    for node_count, row_count in shapes:
        slice_rows = row_count // OWNERS
        portion = owner_grid[:, :, offset:offset + node_count * slice_rows].reshape(count_modes, OWNERS, node_count, slice_rows)
        result.append(jnp.transpose(portion, (2, 0, 1, 3)).reshape(node_count, count_modes, row_count))
        offset = offset + node_count * slice_rows
    return result


def mass_apply(flat_rows, mass_vals, mass_cols):
    count_modes = flat_rows.shape[0]
    blocks = lax.optimization_barrier(flat_rows).reshape(count_modes, ALL_BLOCKS, BLOCK)
    picked = blocks[:, mass_cols, :].astype(jnp.float32)
    product = jnp.einsum("mrei,reoi->mro", picked, mass_vals.astype(jnp.float32))
    return product.reshape(count_modes, -1)


def reference(modes_root, modes_mid, modes_low, factor_root, factor_mid, factor_low, update_mid, update_low, map_mid, map_low, mass_vals, mass_cols):
    shapes = ((1, SEP_ROOT), (2, SEP_MID), (4, SEP_LOW))
    count_modes = modes_root.shape[1]
    stacked = owner_order([modes_root, modes_mid, modes_low])
    z_flat = mass_apply(stacked, mass_vals, mass_cols)
    z_levels = level_order(z_flat, shapes)
    factors = (factor_root, factor_mid, factor_low)
    updates = (None, update_mid, update_low)
    row_maps = (None, map_mid, map_low)
    accumulated = jnp.zeros((count_modes, ALL_BLOCKS, BLOCK), jnp.float32)
    forward = [None, None, None]
    for level_depth in (2, 1, 0):
        acc_levels = level_order(accumulated.reshape(count_modes, -1), shapes)
        right_half = lax.optimization_barrier((z_levels[level_depth] - acc_levels[level_depth]).astype(jnp.bfloat16))
        solved = jnp.einsum("nij,nmj->nmi", factors[level_depth].astype(jnp.float32), right_half.astype(jnp.float32))
        forward[level_depth] = solved
        if level_depth > 0:
            solved_half = lax.optimization_barrier(solved.astype(jnp.bfloat16))
            update_term = jnp.einsum("nai,nmi->nma", updates[level_depth].astype(jnp.float32), solved_half.astype(jnp.float32))
            term_blocks = jnp.transpose(update_term, (1, 0, 2)).reshape(count_modes, -1, BLOCK)
            accumulated = accumulated.at[:, row_maps[level_depth].reshape(-1), :].add(term_blocks)
    xb_blocks = jnp.zeros((count_modes, ALL_BLOCKS, BLOCK), jnp.bfloat16)
    outputs = [None, None, None]
    for level_depth in (0, 1, 2):
        residue = forward[level_depth]
        if level_depth > 0:
            node_count = row_maps[level_depth].shape[0]
            gathered = xb_blocks[:, row_maps[level_depth].reshape(-1), :]
            gathered = jnp.transpose(gathered.reshape(count_modes, node_count, -1), (1, 0, 2))
            back_term = jnp.einsum("nai,nma->nmi", updates[level_depth].astype(jnp.float32), gathered.astype(jnp.float32))
            residue = residue - back_term
        right_half = lax.optimization_barrier(residue.astype(jnp.bfloat16))
        solved = jnp.einsum("nij,nmi->nmj", factors[level_depth].astype(jnp.float32), right_half.astype(jnp.float32))
        outputs[level_depth] = solved
        filled = []
        for index_level in range(3):
            if outputs[index_level] is None:
                filled.append(jnp.zeros((shapes[index_level][0], count_modes, shapes[index_level][1]), jnp.float32))
            else:
                filled.append(outputs[index_level])
        xb_blocks = owner_order(filled).astype(jnp.bfloat16).reshape(count_modes, ALL_BLOCKS, BLOCK)
    y_flat = owner_order(outputs)
    my_flat = mass_apply(y_flat.astype(jnp.bfloat16), mass_vals, mass_cols)
    gram_stiff = jnp.dot(y_flat, z_flat.T, precision=lax.Precision.HIGHEST)
    gram_mass = jnp.dot(y_flat, my_flat.T, precision=lax.Precision.HIGHEST)
    return (outputs[0], outputs[1], outputs[2], gram_stiff, gram_mass)
```

```python
import jax
import jax.numpy as jnp
from jax import lax
from jax.sharding import PartitionSpec as P

BLOCK = 128
F32 = jnp.float32
BF16 = jnp.bfloat16


def scatter_sum(pieces, axis):
    got = lax.all_to_all(pieces.astype(BF16), axis, 0, 0)
    return jnp.sum(got.astype(F32), axis=0)


def gather(piece, axis):
    copies = jnp.broadcast_to(piece[None], (lax.axis_size(axis), *piece.shape))
    return lax.all_to_all(copies, axis, 0, 0)


def neighbours(flat):
    count = lax.axis_size("subtree")
    before = lax.ppermute(flat, "subtree", [(i, i + 1) for i in range(count - 1)])
    after = lax.ppermute(flat, "subtree", [(i + 1, i) for i in range(count - 1)])
    return jnp.concatenate([before, flat, after], axis=1)


def mass_partial(flat, mass_vals, mass_cols, owner):
    modes, rows = flat.shape
    blocks = neighbours(flat).reshape(modes, -1, BLOCK)
    column = mass_cols - (owner - 1) * (rows // BLOCK)
    picked = blocks[:, column, :]
    product = jnp.einsum("mrei,reoi->mro", picked, mass_vals, preferred_element_type=F32)
    return product.reshape(modes, rows)


def flatten(levels):
    return jnp.concatenate(
        [jnp.transpose(part, (1, 0, 2)).reshape(part.shape[1], -1) for part in levels], axis=1
    )


def per_device(
    modes_root,
    modes_mid,
    modes_low,
    factor_root,
    factor_mid,
    factor_low,
    update_mid,
    update_low,
    map_mid,
    map_low,
    mass_vals,
    mass_cols,
):
    owner = lax.axis_index("subtree")
    fronts = lax.axis_size("front")
    owners = lax.axis_size("subtree")
    modes = modes_root.shape[1]
    mine = modes // fronts
    counts = [(part.shape[0], part.shape[2]) for part in (modes_root, modes_mid, modes_low)]
    widths = [n * rows for n, rows in counts]
    starts = [0, widths[0], widths[0] + widths[1]]
    local_blocks = sum(widths) // BLOCK

    def level(piece, depth):
        return piece[:, starts[depth] : starts[depth] + widths[depth]]

    def right_side(piece):
        return gather(piece.astype(BF16), "front").reshape(modes, -1)

    def times_factor(factor, flat):
        n, _, cols = factor.shape
        part = jnp.einsum(
            "nij,mnj->nmi", factor, flat.reshape(modes, n, cols), preferred_element_type=F32
        )
        return scatter_sum(part.reshape(owners, n * modes // owners, -1), "subtree")

    def whole(piece, n):
        return gather(piece.astype(BF16), "subtree").reshape(n, modes, -1)

    def times_update(update, y):
        n = update.shape[0]
        part = jnp.einsum("nai,nmi->nma", update, y, preferred_element_type=F32)
        part = jnp.transpose(part.reshape(n, fronts, mine, BLOCK), (1, 0, 2, 3))
        return scatter_sum(part.reshape(fronts, n * mine, BLOCK), "front").reshape(n, mine, BLOCK)

    def scattered(term, row_map):
        target = row_map.reshape(-1) - owner * local_blocks
        onehot = (target[:, None] == lax.iota(jnp.int32, local_blocks)[None, :]).astype(F32)
        spread = term[:, :, None, :] * onehot[:, None, :, None]
        return jnp.sum(spread, axis=0).reshape(mine, local_blocks * BLOCK)

    def back_term(update, row_map, xb):
        n = update.shape[0]
        target = row_map.reshape(-1) - owner * local_blocks
        here = xb.shape[1] // BLOCK
        onehot = target[:, None] == lax.iota(jnp.int32, here)[None, :]
        blocks = xb.reshape(modes, here, BLOCK)
        g = jnp.zeros((n, modes, BLOCK), BF16)
        for index in range(here):
            g = jnp.where(onehot[:, index][:, None, None], blocks[None, :, index, :], g)
        part = jnp.einsum("nai,nma->nmi", update, g, preferred_element_type=F32)
        return scatter_sum(part.reshape(owners, n * modes // owners, -1), "subtree")

    def times_transposed(factor, d):
        part = jnp.einsum("nij,nmi->nmj", factor, d, preferred_element_type=F32)
        n, _, cols = part.shape
        part = jnp.transpose(part.reshape(n, fronts, mine, cols), (1, 0, 2, 3))
        got = scatter_sum(part.reshape(fronts, n * mine, cols), "front").reshape(n, mine, cols)
        return jnp.transpose(got, (1, 0, 2)).reshape(mine, n * cols)

    stacked = flatten((modes_root, modes_mid, modes_low))
    z_part = mass_partial(stacked, mass_vals, mass_cols, owner)
    z = scatter_sum(z_part.reshape(fronts, mine, -1), "front")

    y_low = times_factor(factor_low, right_side(level(z, 2)))
    acc = scattered(times_update(update_low, whole(y_low, counts[2][0])), map_low)
    y_mid = times_factor(factor_mid, right_side(level(z, 1) - level(acc, 1)))
    acc = acc + scattered(times_update(update_mid, whole(y_mid, counts[1][0])), map_mid)
    y_root = times_factor(factor_root, right_side(level(z, 0) - level(acc, 0)))

    xb = right_side(times_transposed(factor_root, whole(y_root, 1)))
    d_mid = y_mid - back_term(update_mid, map_mid, xb)
    xb_mid = right_side(times_transposed(factor_mid, whole(d_mid, counts[1][0])))
    xb = jnp.concatenate([xb, xb_mid], axis=1)
    d_low = y_low - back_term(update_low, map_low, xb)
    xb_low = right_side(times_transposed(factor_low, whole(d_low, counts[2][0])))
    xb = jnp.concatenate([xb, xb_low], axis=1)

    my_part = mass_partial(xb, mass_vals, mass_cols, owner)
    mass_part = jnp.einsum("kr,jr->kj", my_part.astype(BF16), xb, preferred_element_type=F32)
    got = lax.all_to_all(mass_part.reshape(fronts, mine, modes), "front", 0, 0)
    mass_mine = jnp.sum(got, axis=0)
    stiff_mine = jnp.einsum("kr,jr->kj", z.astype(BF16), xb, preferred_element_type=F32)
    grams = jnp.concatenate([stiff_mine, mass_mine], axis=1)
    grams = jnp.sum(gather(grams, "subtree"), axis=0)
    grams = gather(grams, "front").reshape(modes, 2 * modes)
    outputs = [
        jnp.transpose(level(xb, depth).reshape(modes, n, rows), (1, 0, 2)).astype(F32)
        for depth, (n, rows) in enumerate(counts)
    ]
    return (*outputs, grams[:, :modes].T, grams[:, modes:].T)


def solution(mesh):
    placed = (
        P(None, None, "subtree"),
        P(None, None, "subtree"),
        P(None, None, "subtree"),
        P(None, "front", "subtree"),
        P(None, "front", "subtree"),
        P(None, "front", "subtree"),
        P(None, "subtree", "front"),
        P(None, "subtree", "front"),
        P(None, "subtree"),
        P(None, "subtree"),
        P("subtree", "front", None, None),
        P("subtree", "front"),
    )
    return jax.shard_map(
        per_device,
        mesh=mesh,
        in_specs=placed,
        out_specs=(
            P(None, None, "subtree"),
            P(None, None, "subtree"),
            P(None, None, "subtree"),
            P(),
            P(),
        ),
        check_vma=False,
    )
```

```python
import jax
import jax.numpy as jnp
from jax import lax
from jax.sharding import Mesh, PartitionSpec as P

BLOCK = 128
F32 = jnp.float32
BF16 = jnp.bfloat16
FRONT = ("z", "core")


def total(parts):
    return jnp.sum(parts.astype(F32), axis=0)


def gather(piece, axis):
    copies = jnp.broadcast_to(piece[None], (lax.axis_size(axis), *piece.shape))
    return lax.all_to_all(copies, axis, 0, 0)


def scatter_sum(pieces, axis):
    return total(lax.all_to_all(pieces.astype(BF16), axis, 0, 0))


def full_sum(part, axis):
    return total(gather(part.astype(BF16), axis))


def swap(value):
    return lax.ppermute(value, "core", [(0, 1), (1, 0)])


def neighbours(flat):
    count = lax.axis_size("subtree")
    before = lax.ppermute(flat, "subtree", [(i, i + 1) for i in range(count - 1)])
    after = lax.ppermute(flat, "subtree", [(i + 1, i) for i in range(count - 1)])
    return before, after


def mass_partial(window, column, mass_vals):
    modes = window.shape[0]
    picked = window.reshape(modes, -1, BLOCK)[:, column, :]
    product = jnp.einsum("mrei,reoi->mro", picked, mass_vals, preferred_element_type=F32)
    return product.reshape(modes, -1)


def flatten(levels):
    return jnp.concatenate(
        [jnp.transpose(part, (1, 0, 2)).reshape(part.shape[1], -1) for part in levels], axis=1
    )


def per_device(
    modes_root,
    modes_mid,
    modes_low,
    factor_root,
    factor_mid,
    factor_low,
    update_mid,
    update_low,
    map_mid,
    map_low,
    mass_vals,
    mass_cols,
):
    owner = lax.axis_index("subtree")
    core = lax.axis_index("core")
    owners = lax.axis_size("subtree")
    layers = lax.axis_size("z")
    modes = modes_root.shape[1]
    w_root, w_mid, w_low = modes_root.shape[2], modes_mid.shape[2], modes_low.shape[2]
    b_root, b_mid, b_low = w_root // BLOCK, w_mid // BLOCK, w_low // BLOCK
    local_blocks = b_root + 2 * b_mid + 4 * b_low
    b_own = b_mid + 2 * b_low
    w_own = b_own * BLOCK
    mid_at, low_at = w_root, w_root + w_mid

    def half(value, which, axis=0):
        size = value.shape[axis] // 2
        return lax.dynamic_slice_in_dim(value, which * size, size, axis)

    weights = (factor_low, factor_mid, update_low, update_mid)
    width = factor_low.shape[2]

    def narrow(value):
        flat = value.reshape(-1, value.shape[2])
        return [flat[:, i : i + width] for i in range(0, flat.shape[1], width)]

    sent = jnp.concatenate([piece for w in weights for piece in narrow(half(w, 1 - core))], axis=0)
    received = swap(sent)
    stacks = []
    offset = 0
    for w in weights:
        own = half(w, core)
        rows = own.shape[0] * own.shape[1]
        pieces = []
        for _ in range(0, w.shape[2], width):
            pieces.append(received[offset : offset + rows])
            offset += rows
        other = jnp.concatenate(pieces, axis=1).reshape(own.shape)
        stacks.append(jnp.stack([own, other]))
    f_low, f_mid, u_low, u_mid = stacks

    t_mid = half(map_mid, core)[:, 0] - owner * local_blocks
    t_low = half(map_low, core)[:, 0] - owner * local_blocks
    first_mid = b_root + core * b_mid

    def forward(stack, right):
        part = jnp.einsum("hnij,mnj->hnmi", stack, right, preferred_element_type=F32)
        return scatter_sum(part.reshape(owners, -1, part.shape[-1]), "subtree")

    def whole(piece, shape):
        return gather(piece.astype(BF16), "subtree").reshape(shape)

    def update_term(stack, y):
        part = jnp.einsum("hnai,hnmi->nma", stack, y, preferred_element_type=F32)
        return full_sum(part, "z")

    def placed(term, target, start, count):
        blocks = []
        for index in range(count):
            hit = (target == start + index)[:, None, None]
            blocks.append(jnp.sum(jnp.where(hit, term, 0.0), axis=0))
        return jnp.concatenate(blocks, axis=1)

    def back_term(stack, target, candidates):
        g = jnp.zeros((target.shape[0], modes, BLOCK), BF16)
        for number, block in candidates:
            g = jnp.where((target == number)[:, None, None], block[None], g)
        part = jnp.einsum("hnai,nma->hnmi", stack, g, preferred_element_type=F32)
        return scatter_sum(part.reshape(owners, -1, part.shape[-1]), "subtree")

    def transposed(stack, d):
        part = jnp.einsum("hnij,hnmi->nmj", stack, d, preferred_element_type=F32)
        return full_sum(jnp.transpose(part, (1, 0, 2)).reshape(modes, -1), "z")

    stacked = flatten((modes_root, modes_mid, modes_low))
    before, after = neighbours(stacked)
    column = mass_cols - (owner - 1) * local_blocks
    window = jnp.concatenate([before, stacked, after], axis=1)
    z_part = mass_partial(window, column, mass_vals).astype(BF16)

    def of_core(flat, which):
        mid = w_root + which * w_mid
        low = w_root + 2 * w_mid + which * 2 * w_low
        return jnp.concatenate(
            [flat[:, :w_root], flat[:, mid : mid + w_mid], flat[:, low : low + 2 * w_low]], axis=1
        )

    z_part = jnp.stack([of_core(z_part, 0), of_core(z_part, 1)]).reshape(
        2, layers, modes // layers, w_root + w_own
    )
    z_part = jnp.transpose(z_part, (1, 0, 2, 3)).reshape(2 * layers, *z_part.shape[2:])
    z_mine = scatter_sum(z_part, FRONT)
    z = gather(z_mine.astype(BF16), "z").reshape(modes, -1)

    y_low = forward(f_low, z[:, low_at:].reshape(modes, 2, w_low))
    term = update_term(u_low, whole(y_low, (2, 2, modes, -1)))
    acc_mid = placed(term, t_low, first_mid, b_mid)
    acc_root = placed(term, t_low, 0, b_root)
    right = (z[:, mid_at:low_at].astype(F32) - acc_mid).astype(BF16)
    y_mid = forward(f_mid, right.reshape(modes, 1, w_mid))
    term = update_term(u_mid, whole(y_mid, (2, 1, modes, -1)))
    acc_root = acc_root + placed(term, t_mid, 0, b_root)
    acc_root = acc_root + swap(acc_root)
    right = (z[:, :mid_at].astype(F32) - acc_root).astype(BF16)
    part = jnp.einsum("ij,mj->mi", factor_root[0], right, preferred_element_type=F32)
    y_root = scatter_sum(part.reshape(owners, modes // owners, -1), "subtree")

    d_root = gather(y_root.astype(BF16), "subtree").reshape(modes, -1)
    part = jnp.einsum("ij,mi->mj", factor_root[0], d_root, preferred_element_type=F32)
    s_root = full_sum(part + swap(part), "z")
    x_root = s_root.astype(BF16)
    candidates = [(i, x_root[:, i * BLOCK : (i + 1) * BLOCK]) for i in range(b_root)]
    d_mid = y_mid - back_term(u_mid, t_mid, candidates)
    x_mid = transposed(f_mid, whole(d_mid, (2, 1, modes, -1))).astype(BF16)
    candidates += [(first_mid + i, x_mid[:, i * BLOCK : (i + 1) * BLOCK]) for i in range(b_mid)]
    d_low = y_low - back_term(u_low, t_low, candidates)
    x_low = transposed(f_low, whole(d_low, (2, 2, modes, -1))).astype(BF16)

    y_own = jnp.concatenate([x_root, x_mid, x_low], axis=1)
    before, after = neighbours(y_own)
    others = swap(jnp.concatenate([part[:, w_root:] for part in (before, y_own, after)], axis=1))
    window = jnp.concatenate([before, y_own, after, others], axis=1)
    place = column // local_blocks
    block = column % local_blocks
    is_low = block >= b_root + 2 * b_mid
    after_root = block - b_root
    low_block = after_root - 2 * b_mid
    of = jnp.where(is_low, low_block // (2 * b_low), after_root // b_mid)
    within = jnp.where(is_low, b_mid + low_block % (2 * b_low), after_root % b_mid)
    b_window = b_root + b_own
    mine = jnp.where(block < b_root, block, b_root + within) + place * b_window
    theirs = 3 * b_window + place * b_own + within
    column = jnp.where((block < b_root) | (of == core), mine, theirs)
    my_part = mass_partial(window, column, mass_vals).astype(BF16)

    other = others[:, w_own : 2 * w_own]
    own = y_own[:, w_root:]
    first = jnp.where(core == 0, own, other)
    second = jnp.where(core == 0, other, own)
    y_all = jnp.concatenate(
        [x_root, first[:, :w_mid], second[:, :w_mid], first[:, w_mid:], second[:, w_mid:]], axis=1
    )

    mass_part = jnp.einsum("kr,jr->kj", my_part, y_all, preferred_element_type=F32)
    rows = lax.broadcasted_iota(jnp.int32, z_mine.shape, 1)
    z_mine = jnp.where((core == 0) | (rows >= w_root), z_mine, 0.0).astype(BF16)
    stiff_part = jnp.einsum("kr,jr->kj", z_mine, y_own, preferred_element_type=F32)

    def paired(value):
        size = value.shape[0] // 2
        return jnp.concatenate([value[:size], value[size:]], axis=1)

    n_mass, n_stiff = modes // 2, modes // layers // 2
    spare = jnp.zeros((-(n_mass + n_stiff) % 8, 2 * modes), F32)
    grams = jnp.concatenate([paired(mass_part), paired(stiff_part), spare], axis=0)
    grams = full_sum(grams, "subtree")
    grams = gather(grams.astype(BF16), FRONT)
    mass = total(grams[:, :n_mass])
    stiff = grams[:, n_mass : n_mass + n_stiff].astype(F32)
    stiff = jnp.sum(stiff.reshape(layers, 2, n_stiff, 2, modes), axis=1)
    stiff = jnp.transpose(stiff, (0, 2, 1, 3)).reshape(modes, modes)
    mass = jnp.concatenate([mass[:, :modes], mass[:, modes:]], axis=0)

    def output(flat, count):
        return jnp.transpose(flat.reshape(modes, count, -1), (1, 0, 2)).astype(F32)

    low_from = w_root + 2 * w_mid
    return (
        s_root[None],
        output(y_all[:, w_root:low_from], 2),
        output(y_all[:, low_from:], 4),
        stiff.T,
        mass.T,
    )


def solution(mesh):
    owners, fronts = mesh.shape["subtree"], mesh.shape["front"]
    split = Mesh(mesh.devices.reshape(owners, fronts // 2, 2), ("subtree", *FRONT))
    factor = P(None, FRONT, "subtree")
    update = P(None, "subtree", FRONT)
    rows = P(None, None, "subtree")
    return jax.shard_map(
        per_device,
        mesh=split,
        in_specs=(
            rows,
            rows,
            rows,
            factor,
            factor,
            factor,
            update,
            update,
            P(None, "subtree"),
            P(None, "subtree"),
            P("subtree", FRONT, None, None),
            P("subtree", FRONT),
        ),
        out_specs=(rows, rows, rows, P(), P()),
        check_vma=False,
    )
```

```python
import functools

import jax
import jax.numpy as jnp
from jax import lax
from jax.experimental import pallas as pl
from jax.experimental.pallas import tpu as pltpu
from jax.sharding import Mesh, PartitionSpec as P

BLOCK = 128
F32 = jnp.float32
BF16 = jnp.bfloat16
FRONT = ("z", "core")


def total(parts):
    return jnp.sum(parts.astype(F32), axis=0)


def exchange(pieces, axis, held):
    return lax.optimization_barrier((lax.all_to_all(pieces, axis, 0, 0), *held))


def gather(piece, axis, *held):
    copies = jnp.broadcast_to(piece[None], (lax.axis_size(axis), *piece.shape))
    return exchange(copies, axis, held)


def scatter_sum(pieces, axis, *held):
    got, *held = exchange(pieces.astype(BF16), axis, held)
    return total(got), *held


def full_sum(part, axis, *held):
    got, *held = gather(part.astype(BF16), axis, *held)
    return total(got), *held


def swap(value):
    return lax.ppermute(value, "core", [(0, 1), (1, 0)])


def neighbours(flat):
    count = lax.axis_size("subtree")
    before = lax.ppermute(flat, "subtree", [(i, i + 1) for i in range(count - 1)])
    after = lax.ppermute(flat, "subtree", [(i + 1, i) for i in range(count - 1)])
    return before, after


def _lanes(width):
    return [slice(at, at + 256) for at in range(0, width, 256)]


def _pack_kernel(core_ref, *refs, count, copies):
    weights, sent, stacks = refs[:count], refs[count], refs[count + 1 : 2 * count + 1]
    sems = refs[-1]
    core = core_ref[0]
    moves = []
    row = 0
    for weight, stack in zip(weights, stacks):
        nodes, rows, width = stack.shape[1:]
        moves.append((weight.at[pl.ds(core * nodes, nodes)], stack.at[0]))
        for node in range(nodes):
            for lanes in _lanes(width):
                source = weight.at[(1 - core) * nodes + node, :, lanes]
                moves.append((source, sent.at[row : row + rows]))
                row += rows
    assert len(moves) == copies
    started = [pltpu.make_async_copy(*move, sems.at[i]) for i, move in enumerate(moves)]
    for copy in started:
        copy.start()
    for copy in started:
        copy.wait()


def _unpack_kernel(received, *refs, count, copies):
    stacks, sems = refs[count : 2 * count], refs[-1]
    moves = []
    row = 0
    for stack in stacks:
        nodes, rows, width = stack.shape[1:]
        for node in range(nodes):
            for lanes in _lanes(width):
                moves.append((received.at[row : row + rows], stack.at[1, node, :, lanes]))
                row += rows
    assert len(moves) == copies
    started = [pltpu.make_async_copy(*move, sems.at[i]) for i, move in enumerate(moves)]
    for copy in started:
        copy.start()
    for copy in started:
        copy.wait()


def split_nodes(*weights):
    count = len(weights)
    shapes = [(2, w.shape[0] // 2, *w.shape[1:]) for w in weights]
    crossing = sum(n * (width // 256) for _, n, _, width in shapes)
    rows = sum(n * r * (width // 256) for _, n, r, width in shapes)
    stack_types = [jax.ShapeDtypeStruct(shape, BF16) for shape in shapes]
    anywhere = pl.BlockSpec(memory_space=pl.ANY)
    sent, *stacks = pl.pallas_call(
        functools.partial(_pack_kernel, count=count, copies=crossing + count),
        out_shape=[jax.ShapeDtypeStruct((rows, 256), BF16), *stack_types],
        in_specs=[pl.BlockSpec(memory_space=pltpu.SMEM)] + [anywhere] * count,
        out_specs=[anywhere] * (count + 1),
        scratch_shapes=[pltpu.SemaphoreType.DMA((crossing + count,))],
        name="pack",
    )(lax.axis_index("core").reshape(1).astype(jnp.int32), *weights)
    received = swap(sent)
    return pl.pallas_call(
        functools.partial(_unpack_kernel, count=count, copies=crossing),
        out_shape=stack_types,
        in_specs=[anywhere] * (count + 1),
        out_specs=[anywhere] * count,
        input_output_aliases={i + 1: i for i in range(count)},
        scratch_shapes=[pltpu.SemaphoreType.DMA((crossing,))],
        name="unpack",
    )(received, *stacks)


def mass_partial(window, column, mass_vals):
    modes = window.shape[0]
    picked = window.reshape(modes, -1, BLOCK)[:, column, :]
    product = jnp.einsum("mrei,reoi->mro", picked, mass_vals, preferred_element_type=F32)
    return product.reshape(modes, -1)


def flatten(levels):
    return jnp.concatenate(
        [jnp.transpose(part, (1, 0, 2)).reshape(part.shape[1], -1) for part in levels], axis=1
    )


def per_device(
    modes_root,
    modes_mid,
    modes_low,
    factor_root,
    factor_mid,
    factor_low,
    update_mid,
    update_low,
    map_mid,
    map_low,
    mass_vals,
    mass_cols,
):
    owner = lax.axis_index("subtree")
    core = lax.axis_index("core")
    owners = lax.axis_size("subtree")
    layers = lax.axis_size("z")
    modes = modes_root.shape[1]
    w_root, w_mid, w_low = modes_root.shape[2], modes_mid.shape[2], modes_low.shape[2]
    b_root, b_mid, b_low = w_root // BLOCK, w_mid // BLOCK, w_low // BLOCK
    local_blocks = b_root + 2 * b_mid + 4 * b_low
    b_own = b_mid + 2 * b_low
    w_own = b_own * BLOCK
    mid_at, low_at = w_root, w_root + w_mid

    def half(value, which, axis=0):
        size = value.shape[axis] // 2
        return lax.dynamic_slice_in_dim(value, which * size, size, axis)

    f_low, f_mid, u_low, u_mid = split_nodes(factor_low, factor_mid, update_low, update_mid)

    column = mass_cols - (owner - 1) * local_blocks
    place = column // local_blocks
    block = column % local_blocks
    is_low = block >= b_root + 2 * b_mid
    after_root = block - b_root
    low_block = after_root - 2 * b_mid
    of = jnp.where(is_low, low_block // (2 * b_low), after_root // b_mid)
    within = jnp.where(is_low, b_mid + low_block % (2 * b_low), after_root % b_mid)
    b_window = b_root + b_own
    mine = jnp.where(block < b_root, block, b_root + within) + place * b_window
    theirs = 3 * b_window + place * b_own + within
    column_after = jnp.where((block < b_root) | (of == core), mine, theirs)
    t_mid = half(map_mid, core)[:, 0] - owner * local_blocks
    t_low = half(map_low, core)[:, 0] - owner * local_blocks
    first_mid = b_root + core * b_mid

    def forward(stack, right, *held):
        part = jnp.einsum("hnij,mnj->hnmi", stack, right, preferred_element_type=F32)
        return scatter_sum(part.reshape(owners, -1, part.shape[-1]), "subtree", *held)

    def whole(piece, shape, *held):
        got, *held = gather(piece.astype(BF16), "subtree", *held)
        return got.reshape(shape), *held

    def update_term(stack, y, *held):
        part = jnp.einsum("hnai,hnmi->nma", stack, y, preferred_element_type=F32)
        return full_sum(part, "z", *held)

    def placed(term, target, start, count):
        blocks = []
        for index in range(count):
            hit = (target == start + index)[:, None, None]
            blocks.append(jnp.sum(jnp.where(hit, term, 0.0), axis=0))
        return jnp.concatenate(blocks, axis=1)

    def back_term(stack, target, candidates, *held):
        g = jnp.zeros((target.shape[0], modes, BLOCK), BF16)
        for number, block in candidates:
            g = jnp.where((target == number)[:, None, None], block[None], g)
        part = jnp.einsum("hnai,nma->hnmi", stack, g, preferred_element_type=F32)
        return scatter_sum(part.reshape(owners, -1, part.shape[-1]), "subtree", *held)

    def transposed(stack, d, *held):
        part = jnp.einsum("hnij,hnmi->nmj", stack, d, preferred_element_type=F32)
        return full_sum(jnp.transpose(part, (1, 0, 2)).reshape(modes, -1), "z", *held)

    def cut(flat, start, count):
        return [(start + i, flat[:, i * BLOCK : (i + 1) * BLOCK]) for i in range(count)]

    stacked = flatten((modes_root, modes_mid, modes_low))
    before, after = neighbours(stacked)
    window = jnp.concatenate([before, stacked, after], axis=1)
    z_part = mass_partial(window, column, mass_vals).astype(BF16)

    def of_core(flat, which):
        mid = w_root + which * w_mid
        low = w_root + 2 * w_mid + which * 2 * w_low
        return jnp.concatenate(
            [flat[:, :w_root], flat[:, mid : mid + w_mid], flat[:, low : low + 2 * w_low]], axis=1
        )

    z_part = jnp.stack([of_core(z_part, 0), of_core(z_part, 1)]).reshape(
        2, layers, modes // layers, w_root + w_own
    )
    z_part = jnp.transpose(z_part, (1, 0, 2, 3)).reshape(2 * layers, *z_part.shape[2:])
    z_part, f_low, f_mid, u_low, u_mid, t_mid, t_low, column_after, first_mid = (
        lax.optimization_barrier(
            (z_part, f_low, f_mid, u_low, u_mid, t_mid, t_low, column_after, first_mid)
        )
    )
    (z_mine,) = scatter_sum(z_part, FRONT)
    (z,) = gather(z_mine.astype(BF16), "z")
    z = z.reshape(modes, -1)

    right = z[:, low_at:].reshape(modes, 2, w_low)
    y_low, z, t_low = forward(f_low, right, z, t_low)
    y, z, t_low = whole(y_low, (2, 2, modes, -1), z, t_low)
    term, z, t_low = update_term(u_low, y, z, t_low)
    acc_mid = placed(term, t_low, first_mid, b_mid)
    acc_root = placed(term, t_low, 0, b_root)
    right = (z[:, mid_at:low_at].astype(F32) - acc_mid).astype(BF16)
    right, acc_root = lax.optimization_barrier((right, acc_root))
    y_mid, z, t_mid = forward(f_mid, right.reshape(modes, 1, w_mid), z, t_mid)
    y, z, t_mid = whole(y_mid, (2, 1, modes, -1), z, t_mid)
    term, z, t_mid, acc_root = update_term(u_mid, y, z, t_mid, acc_root)
    acc_root = acc_root + placed(term, t_mid, 0, b_root)
    acc_root = acc_root + swap(acc_root)
    right = (z[:, :mid_at].astype(F32) - acc_root).astype(BF16)
    part = jnp.einsum("ij,mj->mi", factor_root[0], right, preferred_element_type=F32)
    (y_root,) = scatter_sum(part.reshape(owners, modes // owners, -1), "subtree")

    (d_root,) = gather(y_root.astype(BF16), "subtree")
    d_root = d_root.reshape(modes, -1)
    part = jnp.einsum("ij,mi->mj", factor_root[0], d_root, preferred_element_type=F32)
    s_root, z, t_mid = full_sum(part + swap(part), "z", z, t_mid)
    x_root = s_root.astype(BF16)
    v_mid, y_mid, x_root = back_term(u_mid, t_mid, cut(x_root, 0, b_root), y_mid, x_root)
    d_mid, x_root = whole(y_mid - v_mid, (2, 1, modes, -1), x_root)
    s_mid, x_root, t_low, first_mid = transposed(f_mid, d_mid, x_root, t_low, first_mid)
    x_mid = s_mid.astype(BF16)
    candidates = cut(x_root, 0, b_root) + cut(x_mid, first_mid, b_mid)
    v_low, y_low, x_mid, x_root = back_term(u_low, t_low, candidates, y_low, x_mid, x_root)
    d_low, x_mid, x_root = whole(y_low - v_low, (2, 2, modes, -1), x_mid, x_root)
    s_low, x_mid, x_root, z, s_root = transposed(f_low, d_low, x_mid, x_root, z, s_root)
    x_low = s_low.astype(BF16)

    y_own = jnp.concatenate([x_root, x_mid, x_low], axis=1)
    before, after = neighbours(y_own)
    others = swap(jnp.concatenate([part[:, w_root:] for part in (before, y_own, after)], axis=1))
    window = jnp.concatenate([before, y_own, after, others], axis=1)
    my_part = mass_partial(window, column_after, mass_vals).astype(BF16)

    other = others[:, w_own : 2 * w_own]
    own = y_own[:, w_root:]
    first = jnp.where(core == 0, own, other)
    second = jnp.where(core == 0, other, own)
    y_all = jnp.concatenate(
        [x_root, first[:, :w_mid], second[:, :w_mid], first[:, w_mid:], second[:, w_mid:]], axis=1
    )

    mass_part = jnp.einsum("jr,kr->jk", y_all, my_part, preferred_element_type=F32)
    size = modes // layers
    y_mine = lax.dynamic_slice_in_dim(y_own, lax.axis_index("z") * size, size, axis=0)
    rows = lax.broadcasted_iota(jnp.int32, y_mine.shape, 1)
    y_mine = jnp.where((core == 0) | (rows >= w_root), y_mine, 0).astype(BF16)
    stiff_part = jnp.einsum("jr,kr->jk", y_mine, z, preferred_element_type=F32)

    def paired(value):
        size = value.shape[0] // 2
        return jnp.concatenate([value[:size], value[size:]], axis=1)

    n_mass, n_stiff = modes // 2, size // 2
    spare = jnp.zeros((-(n_mass + n_stiff) % 8, 2 * modes), F32)
    grams = jnp.concatenate([paired(mass_part), paired(stiff_part), spare], axis=0)
    grams, y_all, s_root = full_sum(grams, "subtree", y_all, s_root)
    (grams,) = gather(grams.astype(BF16), FRONT)
    mass = total(grams[:, :n_mass])
    stiff = grams[:, n_mass : n_mass + n_stiff].astype(F32)
    stiff = jnp.sum(stiff.reshape(layers, 2, n_stiff, 2, modes), axis=1)
    stiff = jnp.transpose(stiff, (0, 2, 1, 3)).reshape(modes, modes)
    mass = jnp.concatenate([mass[:, :modes], mass[:, modes:]], axis=0)

    def output(flat, count):
        return jnp.transpose(flat.reshape(modes, count, -1), (1, 0, 2)).astype(F32)

    low_from = w_root + 2 * w_mid
    return (
        s_root[None],
        output(y_all[:, w_root:low_from], 2),
        output(y_all[:, low_from:], 4),
        stiff,
        mass,
    )


def solution(mesh):
    owners, fronts = mesh.shape["subtree"], mesh.shape["front"]
    split = Mesh(mesh.devices.reshape(owners, fronts // 2, 2), ("subtree", *FRONT))
    factor = P(None, FRONT, "subtree")
    update = P(None, "subtree", FRONT)
    rows = P(None, None, "subtree")
    return jax.shard_map(
        per_device,
        mesh=split,
        in_specs=(
            rows,
            rows,
            rows,
            factor,
            factor,
            factor,
            update,
            update,
            P(None, "subtree"),
            P(None, "subtree"),
            P("subtree", FRONT, None, None),
            P("subtree", FRONT),
        ),
        out_specs=(rows, rows, rows, P(), P()),
        check_vma=False,
    )
```

```python
import functools

import jax
import jax.numpy as jnp
from jax import lax
from jax.experimental import pallas as pl
from jax.experimental.pallas import tpu as pltpu
from jax.sharding import Mesh, PartitionSpec as P

BLOCK = 128
F32 = jnp.float32
BF16 = jnp.bfloat16
FRONT = ("z", "core")


def total(parts):
    return jnp.sum(parts.astype(F32), axis=0)


def exchange(pieces, axis, held):
    return lax.optimization_barrier((lax.all_to_all(pieces, axis, 0, 0), *held))


def gather(piece, axis, *held):
    copies = jnp.broadcast_to(piece[None], (lax.axis_size(axis), *piece.shape))
    return exchange(copies, axis, held)


def scatter_sum(pieces, axis, *held):
    got, *held = exchange(pieces.astype(BF16), axis, held)
    return total(got), *held


def full_sum(part, axis, *held):
    got, *held = gather(part.astype(BF16), axis, *held)
    return total(got), *held


def swap(value):
    return lax.ppermute(value, "core", [(0, 1), (1, 0)])


def neighbours(flat):
    count = lax.axis_size("subtree")
    before = lax.ppermute(flat, "subtree", [(i, i + 1) for i in range(count - 1)])
    after = lax.ppermute(flat, "subtree", [(i + 1, i) for i in range(count - 1)])
    return before, after


def _lanes(width):
    return [slice(at, at + 256) for at in range(0, width, 256)]


def _run(moves, sems):
    copies = [pltpu.make_async_copy(*move, sems.at[i]) for i, move in enumerate(moves)]
    for copy in copies:
        copy.start()
    for copy in copies:
        copy.wait()


def _pack_kernel(core_ref, *refs, count):
    weights, sent, stacks = refs[:count], refs[count], refs[count + 1 : 2 * count + 1]
    staged, halves, sems = refs[2 * count + 1], refs[2 * count + 2 : -1], refs[-1]
    core = core_ref[0]
    moves = []
    row = 0
    for weight, half in zip(weights, halves):
        nodes, rows, width = half.shape
        moves.append((weight.at[pl.ds(core * nodes, nodes)], half))
        for node in range(nodes):
            for lanes in _lanes(width):
                source = weight.at[(1 - core) * nodes + node, :, lanes]
                moves.append((source, staged.at[row : row + rows]))
                row += rows
    _run(moves, sems)
    out = [(half, stack.at[0]) for half, stack in zip(halves, stacks)]
    _run([(staged, sent), *out], sems)


def _unpack_kernel(received, *refs, count):
    stacks, staged, sems = refs[count : 2 * count], refs[-2], refs[-1]
    _run([(received, staged)], sems)
    moves = []
    row = 0
    for stack in stacks:
        nodes, rows, width = stack.shape[1:]
        for node in range(nodes):
            for lanes in _lanes(width):
                moves.append((staged.at[row : row + rows], stack.at[1, node, :, lanes]))
                row += rows
    _run(moves, sems)


def split_nodes(*weights):
    count = len(weights)
    shapes = [(2, w.shape[0] // 2, *w.shape[1:]) for w in weights]
    crossing = sum(n * (width // 256) for _, n, _, width in shapes)
    rows = sum(n * r * (width // 256) for _, n, r, width in shapes)
    stack_types = [jax.ShapeDtypeStruct(shape, BF16) for shape in shapes]
    anywhere = pl.BlockSpec(memory_space=pl.ANY)
    sent, *stacks = pl.pallas_call(
        functools.partial(_pack_kernel, count=count),
        out_shape=[jax.ShapeDtypeStruct((rows, 256), BF16), *stack_types],
        in_specs=[pl.BlockSpec(memory_space=pltpu.SMEM)] + [anywhere] * count,
        out_specs=[anywhere] * (count + 1),
        scratch_shapes=[
            pltpu.VMEM((rows, 256), BF16),
            *(pltpu.VMEM(shape[1:], BF16) for shape in shapes),
            pltpu.SemaphoreType.DMA((crossing + count,)),
        ],
        name="pack",
    )(lax.axis_index("core").reshape(1).astype(jnp.int32), *weights)
    received = swap(sent)
    return pl.pallas_call(
        functools.partial(_unpack_kernel, count=count),
        out_shape=stack_types,
        in_specs=[anywhere] * (count + 1),
        out_specs=[anywhere] * count,
        input_output_aliases={i + 1: i for i in range(count)},
        scratch_shapes=[pltpu.VMEM((rows, 256), BF16), pltpu.SemaphoreType.DMA((crossing,))],
        name="unpack",
    )(received, *stacks)


def to_pieces(value, count, width):
    lead = value.size // value.shape[-1] // 8
    blocks = value.reshape(lead, 8, -1, width).transpose(0, 2, 1, 3).reshape(-1, 8, width)
    spare = count - blocks.shape[0]
    if spare:
        blocks = jnp.concatenate([blocks, jnp.zeros((spare, 8, width), blocks.dtype)], axis=0)
    return blocks


def from_pieces(blocks, shape):
    width = blocks.shape[-1]
    across = shape[-1] // width
    lead = 1
    for size in shape[:-1]:
        lead *= size
    used = blocks[: lead // 8 * across]
    return used.reshape(lead // 8, across, 8, width).transpose(0, 2, 1, 3).reshape(shape)


def mass_partial(window, column, mass_vals):
    modes = window.shape[0]
    picked = window.reshape(modes, -1, BLOCK)[:, column, :]
    product = jnp.einsum("mrei,reoi->mro", picked, mass_vals, preferred_element_type=F32)
    return product.reshape(modes, -1)


def flatten(levels):
    return jnp.concatenate(
        [jnp.transpose(part, (1, 0, 2)).reshape(part.shape[1], -1) for part in levels], axis=1
    )


def per_device(
    modes_root,
    modes_mid,
    modes_low,
    factor_root,
    factor_mid,
    factor_low,
    update_mid,
    update_low,
    map_mid,
    map_low,
    mass_vals,
    mass_cols,
):
    owner = lax.axis_index("subtree")
    core = lax.axis_index("core")
    owners = lax.axis_size("subtree")
    layers = lax.axis_size("z")
    modes = modes_root.shape[1]
    w_root, w_mid, w_low = modes_root.shape[2], modes_mid.shape[2], modes_low.shape[2]
    b_root, b_mid, b_low = w_root // BLOCK, w_mid // BLOCK, w_low // BLOCK
    local_blocks = b_root + 2 * b_mid + 4 * b_low
    b_own = b_mid + 2 * b_low
    w_own = b_own * BLOCK
    mid_at, low_at = w_root, w_root + w_mid

    def half(value, which, axis=0):
        size = value.shape[axis] // 2
        return lax.dynamic_slice_in_dim(value, which * size, size, axis)

    f_low, f_mid, u_low, u_mid = split_nodes(factor_low, factor_mid, update_low, update_mid)

    column = mass_cols - (owner - 1) * local_blocks
    place = column // local_blocks
    block = column % local_blocks
    is_low = block >= b_root + 2 * b_mid
    after_root = block - b_root
    low_block = after_root - 2 * b_mid
    of = jnp.where(is_low, low_block // (2 * b_low), after_root // b_mid)
    within = jnp.where(is_low, b_mid + low_block % (2 * b_low), after_root % b_mid)
    b_window = b_root + b_own
    mine = jnp.where(block < b_root, block, b_root + within) + place * b_window
    theirs = 3 * b_window + place * b_own + within
    column_after = jnp.where((block < b_root) | (of == core), mine, theirs)
    t_mid = half(map_mid, core)[:, 0] - owner * local_blocks
    t_low = half(map_low, core)[:, 0] - owner * local_blocks
    first_mid = b_root + core * b_mid

    def forward(stack, right, *held):
        part = jnp.einsum("hnij,mnj->hnmi", stack, right, preferred_element_type=F32)
        width = part.size // owners // 8
        return scatter_sum(to_pieces(part.astype(BF16), owners, width), "subtree", *held)

    def whole(piece, shape, *held):
        got, *held = gather(piece.astype(BF16), "subtree", *held)
        return from_pieces(got, shape), *held

    def update_term(stack, y, *held):
        part = jnp.einsum("hnai,hnmi->nma", stack, y, preferred_element_type=F32)
        return full_sum(part, "z", *held)

    def placed(term, target, start, count):
        blocks = []
        for index in range(count):
            hit = (target == start + index)[:, None, None]
            blocks.append(jnp.sum(jnp.where(hit, term, 0.0), axis=0))
        return jnp.concatenate(blocks, axis=1)

    def back_term(stack, target, candidates, *held):
        g = jnp.zeros((target.shape[0], modes, BLOCK), BF16)
        for number, block in candidates:
            g = jnp.where((target == number)[:, None, None], block[None], g)
        part = jnp.einsum("hnai,nma->hnmi", stack, g, preferred_element_type=F32)
        width = part.size // owners // 8
        return scatter_sum(to_pieces(part.astype(BF16), owners, width), "subtree", *held)

    def transposed(stack, d, *held):
        part = jnp.einsum("hnij,hnmi->nmj", stack, d, preferred_element_type=F32)
        return full_sum(jnp.transpose(part, (1, 0, 2)).reshape(modes, -1), "z", *held)

    def cut(flat, start, count):
        return [(start + i, flat[:, i * BLOCK : (i + 1) * BLOCK]) for i in range(count)]

    stacked = flatten((modes_root, modes_mid, modes_low))
    before, after = neighbours(stacked)
    window = jnp.concatenate([before, stacked, after], axis=1)
    z_part = mass_partial(window, column, mass_vals).astype(BF16)

    def of_core(flat, which):
        mid = w_root + which * w_mid
        low = w_root + 2 * w_mid + which * 2 * w_low
        return jnp.concatenate(
            [flat[:, :w_root], flat[:, mid : mid + w_mid], flat[:, low : low + 2 * w_low]], axis=1
        )

    z_part = jnp.stack([of_core(z_part, 0), of_core(z_part, 1)]).reshape(
        2, layers, modes // layers, w_root + w_own
    )
    z_part = jnp.transpose(z_part, (1, 0, 2, 3)).reshape(2 * layers, *z_part.shape[2:])
    z_part, f_low, f_mid, u_low, u_mid, t_mid, t_low, column_after, first_mid = (
        lax.optimization_barrier(
            (z_part, f_low, f_mid, u_low, u_mid, t_mid, t_low, column_after, first_mid)
        )
    )
    (z_mine,) = scatter_sum(z_part, FRONT)
    (z,) = gather(z_mine.astype(BF16), "z")
    z = z.reshape(modes, -1)

    right = z[:, low_at:].reshape(modes, 2, w_low)
    y_low, z, t_low = forward(f_low, right, z, t_low)
    y, z, t_low = whole(y_low, (2, 2, modes, f_low.shape[-2]), z, t_low)
    term, z, t_low = update_term(u_low, y, z, t_low)
    acc_mid = placed(term, t_low, first_mid, b_mid)
    acc_root = placed(term, t_low, 0, b_root)
    right = (z[:, mid_at:low_at].astype(F32) - acc_mid).astype(BF16)
    right, acc_root = lax.optimization_barrier((right, acc_root))
    y_mid, z, t_mid = forward(f_mid, right.reshape(modes, 1, w_mid), z, t_mid)
    y, z, t_mid = whole(y_mid, (2, 1, modes, f_mid.shape[-2]), z, t_mid)
    term, z, t_mid, acc_root = update_term(u_mid, y, z, t_mid, acc_root)
    acc_root = acc_root + placed(term, t_mid, 0, b_root)
    acc_root = acc_root + swap(acc_root)
    right = (z[:, :mid_at].astype(F32) - acc_root).astype(BF16)
    part = jnp.einsum("ij,mj->mi", factor_root[0], right, preferred_element_type=F32)
    (y_root,) = scatter_sum(to_pieces(part.astype(BF16), owners, 2 * BLOCK), "subtree")

    (d_root,) = whole(y_root, part.shape)
    part = jnp.einsum("ij,mi->mj", factor_root[0], d_root, preferred_element_type=F32)
    s_root, z, t_mid = full_sum(part + swap(part), "z", z, t_mid)
    x_root = s_root.astype(BF16)
    v_mid, y_mid, x_root = back_term(u_mid, t_mid, cut(x_root, 0, b_root), y_mid, x_root)
    d_mid, x_root = whole(y_mid - v_mid, (2, 1, modes, f_mid.shape[-2]), x_root)
    s_mid, x_root, t_low, first_mid = transposed(f_mid, d_mid, x_root, t_low, first_mid)
    x_mid = s_mid.astype(BF16)
    candidates = cut(x_root, 0, b_root) + cut(x_mid, first_mid, b_mid)
    v_low, y_low, x_mid, x_root = back_term(u_low, t_low, candidates, y_low, x_mid, x_root)
    d_low, x_mid, x_root = whole(y_low - v_low, (2, 2, modes, f_low.shape[-2]), x_mid, x_root)
    s_low, x_mid, x_root, z, s_root = transposed(f_low, d_low, x_mid, x_root, z, s_root)
    x_low = s_low.astype(BF16)

    y_own = jnp.concatenate([x_root, x_mid, x_low], axis=1)
    before, after = neighbours(y_own)
    others = swap(jnp.concatenate([part[:, w_root:] for part in (before, y_own, after)], axis=1))
    window = jnp.concatenate([before, y_own, after, others], axis=1)
    my_part = mass_partial(window, column_after, mass_vals).astype(BF16)

    other = others[:, w_own : 2 * w_own]
    own = y_own[:, w_root:]
    first = jnp.where(core == 0, own, other)
    second = jnp.where(core == 0, other, own)
    y_all = jnp.concatenate(
        [x_root, first[:, :w_mid], second[:, :w_mid], first[:, w_mid:], second[:, w_mid:]], axis=1
    )

    mass_part = jnp.einsum("jr,kr->jk", y_all, my_part, preferred_element_type=F32)
    size = modes // layers
    y_mine = lax.dynamic_slice_in_dim(y_own, lax.axis_index("z") * size, size, axis=0)
    rows = lax.broadcasted_iota(jnp.int32, y_mine.shape, 1)
    y_mine = jnp.where((core == 0) | (rows >= w_root), y_mine, 0).astype(BF16)
    stiff_part = jnp.einsum("jr,kr->jk", y_mine, z, preferred_element_type=F32)

    def paired(value):
        size = value.shape[0] // 2
        return jnp.concatenate([value[:size], value[size:]], axis=1)

    n_mass, n_stiff = modes // 2, size // 2
    spare = jnp.zeros((-(n_mass + n_stiff) % 8, 2 * modes), F32)
    grams = jnp.concatenate([paired(mass_part), paired(stiff_part), spare], axis=0)
    grams, y_all, s_root = full_sum(grams, "subtree", y_all, s_root)
    (grams,) = gather(grams.astype(BF16), FRONT)
    mass = total(grams[:, :n_mass])
    stiff = grams[:, n_mass : n_mass + n_stiff].astype(F32)
    stiff = jnp.sum(stiff.reshape(layers, 2, n_stiff, 2, modes), axis=1)
    stiff = jnp.transpose(stiff, (0, 2, 1, 3)).reshape(modes, modes)
    mass = jnp.concatenate([mass[:, :modes], mass[:, modes:]], axis=0)

    def output(flat, count):
        return jnp.transpose(flat.reshape(modes, count, -1), (1, 0, 2)).astype(F32)

    low_from = w_root + 2 * w_mid
    return (
        s_root[None],
        output(y_all[:, w_root:low_from], 2),
        output(y_all[:, low_from:], 4),
        stiff,
        mass,
    )


def solution(mesh):
    owners, fronts = mesh.shape["subtree"], mesh.shape["front"]
    split = Mesh(mesh.devices.reshape(owners, fronts // 2, 2), ("subtree", *FRONT))
    factor = P(None, FRONT, "subtree")
    update = P(None, "subtree", FRONT)
    rows = P(None, None, "subtree")
    return jax.shard_map(
        per_device,
        mesh=split,
        in_specs=(
            rows,
            rows,
            rows,
            factor,
            factor,
            factor,
            update,
            update,
            P(None, "subtree"),
            P(None, "subtree"),
            P("subtree", FRONT, None, None),
            P("subtree", FRONT),
        ),
        out_specs=(rows, rows, rows, P(), P()),
        check_vma=False,
    )
```

```python
import functools

import jax
import jax.numpy as jnp
from jax import lax
from jax.experimental import pallas as pl
from jax.experimental.pallas import tpu as pltpu
from jax.sharding import Mesh, PartitionSpec as P

BLOCK = 128
F32 = jnp.float32
BF16 = jnp.bfloat16
FRONT = ("z", "core")


def total(parts):
    return jnp.sum(parts.astype(F32), axis=0)


def exchange(pieces, axis, held):
    return lax.optimization_barrier((lax.all_to_all(pieces, axis, 0, 0), *held))


def gather(piece, axis, *held):
    copies = jnp.broadcast_to(piece[None], (lax.axis_size(axis), *piece.shape))
    return exchange(copies, axis, held)


def scatter_sum(pieces, axis, *held):
    got, *held = exchange(pieces.astype(BF16), axis, held)
    return total(got), *held


def full_sum(part, axis, *held):
    got, *held = gather(part.astype(BF16), axis, *held)
    return total(got), *held


def swap(value):
    return lax.ppermute(value, "core", [(0, 1), (1, 0)])


def neighbours(flat):
    count = lax.axis_size("subtree")
    before = lax.ppermute(flat, "subtree", [(i, i + 1) for i in range(count - 1)])
    after = lax.ppermute(flat, "subtree", [(i + 1, i) for i in range(count - 1)])
    return before, after


def _lanes(width):
    return [slice(at, at + 256) for at in range(0, width, 256)]


def _run(moves, sems):
    copies = [pltpu.make_async_copy(*move, sems.at[i]) for i, move in enumerate(moves)]
    for copy in copies:
        copy.start()
    for copy in copies:
        copy.wait()


def _pack_kernel(core_ref, *refs, count):
    weights, sent, stacks = refs[:count], refs[count], refs[count + 1 : 2 * count + 1]
    staged, halves, sems = refs[2 * count + 1], refs[2 * count + 2 : -1], refs[-1]
    core = core_ref[0]
    moves = []
    row = 0
    for weight, half in zip(weights, halves):
        nodes, rows, width = half.shape
        moves.append((weight.at[pl.ds(core * nodes, nodes)], half))
        for node in range(nodes):
            for lanes in _lanes(width):
                source = weight.at[(1 - core) * nodes + node, :, lanes]
                moves.append((source, staged.at[row : row + rows]))
                row += rows
    _run(moves, sems)
    out = [(half, stack.at[0]) for half, stack in zip(halves, stacks)]
    _run([(staged, sent), *out], sems)


def _unpack_kernel(received, *refs, count):
    stacks, sems = refs[count : 2 * count], refs[-1]
    moves = []
    row = 0
    for stack in stacks:
        nodes, rows, width = stack.shape[1:]
        for node in range(nodes):
            for lanes in _lanes(width):
                moves.append((received.at[row : row + rows], stack.at[1, node, :, lanes]))
                row += rows
    _run(moves, sems)


def _side_by_side_kernel(*refs):
    levels, flat, sems = refs[:-2], refs[-2], refs[-1]
    moves = []
    at = 0
    for level in levels:
        nodes, _, width = level.shape
        for node in range(nodes):
            moves.append((level.at[node], flat.at[:, at : at + width]))
            at += width
    _run(moves, sems)


def side_by_side(*levels):
    width = sum(level.shape[0] * level.shape[2] for level in levels)
    return pl.pallas_call(
        _side_by_side_kernel,
        out_shape=jax.ShapeDtypeStruct((levels[0].shape[1], width), BF16),
        in_specs=[pl.BlockSpec(memory_space=pl.ANY)] * len(levels),
        out_specs=pl.BlockSpec(memory_space=pltpu.VMEM),
        scratch_shapes=[pltpu.SemaphoreType.DMA((sum(level.shape[0] for level in levels),))],
        name="side_by_side",
    )(*levels)


def split_nodes(*weights):
    count = len(weights)
    shapes = [(2, w.shape[0] // 2, *w.shape[1:]) for w in weights]
    crossing = sum(n * (width // 256) for _, n, _, width in shapes)
    rows = sum(n * r * (width // 256) for _, n, r, width in shapes)
    anywhere = pl.BlockSpec(memory_space=pl.ANY)
    sent, *stacks = pl.pallas_call(
        functools.partial(_pack_kernel, count=count),
        out_shape=[jax.ShapeDtypeStruct(shape, BF16) for shape in ((rows, 256), *shapes)],
        in_specs=[pl.BlockSpec(memory_space=pltpu.SMEM)] + [anywhere] * count,
        out_specs=[anywhere] * (count + 1),
        scratch_shapes=[
            pltpu.VMEM((rows, 256), BF16),
            *(pltpu.VMEM(shape[1:], BF16) for shape in shapes),
            pltpu.SemaphoreType.DMA((crossing + count,)),
        ],
        name="pack",
    )(lax.axis_index("core").reshape(1).astype(jnp.int32), *weights)
    return stacks, swap(sent)


def unpacked(stacks, received):
    count = len(stacks)
    crossing = sum(s.shape[1] * (s.shape[3] // 256) for s in stacks)
    anywhere = pl.BlockSpec(memory_space=pl.ANY)
    return pl.pallas_call(
        functools.partial(_unpack_kernel, count=count),
        out_shape=[jax.ShapeDtypeStruct(s.shape, BF16) for s in stacks],
        in_specs=[pl.BlockSpec(memory_space=pltpu.VMEM)] + [anywhere] * count,
        out_specs=[anywhere] * count,
        input_output_aliases={i + 1: i for i in range(count)},
        scratch_shapes=[pltpu.SemaphoreType.DMA((crossing,))],
        name="unpack",
    )(pltpu.with_memory_space_constraint(received, pltpu.VMEM), *stacks)


def to_pieces(value, count, width):
    lead = value.size // value.shape[-1] // 8
    blocks = value.reshape(lead, 8, -1, width).transpose(0, 2, 1, 3).reshape(-1, 8, width)
    spare = count - blocks.shape[0]
    if spare:
        blocks = jnp.concatenate([blocks, jnp.zeros((spare, 8, width), blocks.dtype)], axis=0)
    return blocks


def from_pieces(blocks, shape):
    width = blocks.shape[-1]
    across = shape[-1] // width
    lead = 1
    for size in shape[:-1]:
        lead *= size
    used = blocks[: lead // 8 * across]
    return used.reshape(lead // 8, across, 8, width).transpose(0, 2, 1, 3).reshape(shape)


def mass_partial(window, column, mass_vals):
    modes = window.shape[0]
    picked = window.reshape(modes, -1, BLOCK)[:, column, :]
    product = jnp.einsum("mrei,reoi->mro", picked, mass_vals, preferred_element_type=F32)
    return product.reshape(modes, -1)


def per_device(
    modes_root,
    modes_mid,
    modes_low,
    factor_root,
    factor_mid,
    factor_low,
    update_mid,
    update_low,
    map_mid,
    map_low,
    mass_vals,
    mass_cols,
):
    owner = lax.axis_index("subtree")
    core = lax.axis_index("core")
    owners = lax.axis_size("subtree")
    layers = lax.axis_size("z")
    modes = modes_root.shape[1]
    w_root, w_mid, w_low = modes_root.shape[2], modes_mid.shape[2], modes_low.shape[2]
    b_root, b_mid, b_low = w_root // BLOCK, w_mid // BLOCK, w_low // BLOCK
    local_blocks = b_root + 2 * b_mid + 4 * b_low
    b_own = b_mid + 2 * b_low
    w_own = b_own * BLOCK
    mid_at, low_at = w_root, w_root + w_mid

    def half(value, which, axis=0):
        size = value.shape[axis] // 2
        return lax.dynamic_slice_in_dim(value, which * size, size, axis)

    stacks, received = split_nodes(factor_low, factor_mid, update_low, update_mid)

    column = mass_cols - (owner - 1) * local_blocks
    place = column // local_blocks
    block = column % local_blocks
    is_low = block >= b_root + 2 * b_mid
    after_root = block - b_root
    low_block = after_root - 2 * b_mid
    of = jnp.where(is_low, low_block // (2 * b_low), after_root // b_mid)
    within = jnp.where(is_low, b_mid + low_block % (2 * b_low), after_root % b_mid)
    b_window = b_root + b_own
    mine = jnp.where(block < b_root, block, b_root + within) + place * b_window
    theirs = 3 * b_window + place * b_own + within
    column_after = jnp.where((block < b_root) | (of == core), mine, theirs)
    t_mid = half(map_mid, core)[:, 0] - owner * local_blocks
    t_low = half(map_low, core)[:, 0] - owner * local_blocks
    first_mid = b_root + core * b_mid

    def forward(stack, right, *held):
        part = jnp.einsum("hnij,mnj->hnmi", stack, right, preferred_element_type=F32)
        width = part.size // owners // 8
        return scatter_sum(to_pieces(part.astype(BF16), owners, width), "subtree", *held)

    def whole(piece, shape, *held):
        got, *held = gather(piece.astype(BF16), "subtree", *held)
        return from_pieces(got, shape), *held

    def update_term(stack, y, *held):
        part = jnp.einsum("hnai,hnmi->nma", stack, y, preferred_element_type=F32)
        return full_sum(part, "z", *held)

    def placed(term, target, count):
        blocks = []
        for index in range(count):
            hit = (target == index)[:, None, None]
            blocks.append(jnp.sum(jnp.where(hit, term, 0.0), axis=0))
        return jnp.concatenate(blocks, axis=1)

    def back_term(stack, candidates, *held):
        g = jnp.zeros((stack.shape[1], modes, BLOCK), BF16)
        for hit, block in candidates:
            g = jnp.where(hit[:, None, None], block[None], g)
        part = jnp.einsum("hnai,nma->hnmi", stack, g, preferred_element_type=F32)
        width = part.size // owners // 8
        return scatter_sum(to_pieces(part.astype(BF16), owners, width), "subtree", *held)

    def transposed(stack, d, *held):
        part = jnp.einsum("hnij,hnmi->nmj", stack, d, preferred_element_type=F32)
        return full_sum(jnp.transpose(part, (1, 0, 2)).reshape(modes, -1), "z", *held)

    def cut(flat, target, count):
        return [(target == i, flat[:, i * BLOCK : (i + 1) * BLOCK]) for i in range(count)]

    stacked = side_by_side(modes_root, modes_mid, modes_low)
    before, after = neighbours(stacked)
    window = jnp.concatenate([before, stacked, after], axis=1)
    z_part = mass_partial(window, column, mass_vals).astype(BF16)

    def of_core(flat, which):
        mid = w_root + which * w_mid
        low = w_root + 2 * w_mid + which * 2 * w_low
        return jnp.concatenate(
            [flat[:, :w_root], flat[:, mid : mid + w_mid], flat[:, low : low + 2 * w_low]], axis=1
        )

    z_part = jnp.stack([of_core(z_part, 0), of_core(z_part, 1)]).reshape(
        2, layers, modes // layers, w_root + w_own
    )
    z_part = jnp.transpose(z_part, (1, 0, 2, 3)).reshape(2 * layers, *z_part.shape[2:])
    layer = lax.axis_index("z")
    t_own = t_low - first_mid
    z_part, received, t_mid, t_low, t_own, column_after, core, layer = lax.optimization_barrier(
        (z_part, received, t_mid, t_low, t_own, column_after, core, layer)
    )
    (z_mine,) = scatter_sum(z_part, FRONT)
    f_low, f_mid, u_low, u_mid = unpacked(stacks, received)
    (z,) = gather(z_mine.astype(BF16), "z")
    z = z.reshape(modes, -1)

    right = z[:, low_at:].reshape(modes, 2, w_low)
    y_low, t_low, t_own = forward(f_low, right, t_low, t_own)
    y, t_low, t_own = whole(y_low, (2, 2, modes, f_low.shape[-2]), t_low, t_own)
    term, t_low, t_own = update_term(u_low, y, t_low, t_own)
    acc_mid = placed(term, t_own, b_mid)
    acc_root = placed(term, t_low, b_root)
    right = (z[:, mid_at:low_at].astype(F32) - acc_mid).astype(BF16)
    right, acc_root = lax.optimization_barrier((right, acc_root))
    y_mid, t_mid = forward(f_mid, right.reshape(modes, 1, w_mid), t_mid)
    y, t_mid = whole(y_mid, (2, 1, modes, f_mid.shape[-2]), t_mid)
    term, t_mid, acc_root = update_term(u_mid, y, t_mid, acc_root)
    acc_root = acc_root + placed(term, t_mid, b_root)
    acc_root = acc_root + swap(acc_root)
    right = (z[:, :mid_at].astype(F32) - acc_root).astype(BF16)
    part = jnp.einsum("ij,mj->mi", factor_root[0], right, preferred_element_type=F32)
    (y_root,) = scatter_sum(to_pieces(part.astype(BF16), owners, 2 * BLOCK), "subtree")

    (d_root,) = whole(y_root, part.shape)
    part = jnp.einsum("ij,mi->mj", factor_root[0], d_root, preferred_element_type=F32)
    s_root, t_mid = full_sum(part + swap(part), "z", t_mid)
    x_root = s_root.astype(BF16)
    root_blocks = cut(x_root, t_mid, b_root)
    v_mid, y_mid, x_root = back_term(u_mid, root_blocks, y_mid, x_root)
    d_mid, x_root = whole(y_mid - v_mid, (2, 1, modes, f_mid.shape[-2]), x_root)
    s_mid, x_root, t_low, t_own = transposed(f_mid, d_mid, x_root, t_low, t_own)
    x_mid = s_mid.astype(BF16)
    blocks = cut(x_root, t_low, b_root) + cut(x_mid, t_own, b_mid)
    v_low, y_low, x_mid, x_root = back_term(u_low, blocks, y_low, x_mid, x_root)
    d_low, x_mid, x_root = whole(y_low - v_low, (2, 2, modes, f_low.shape[-2]), x_mid, x_root)
    s_low, x_mid, x_root, s_root, column_after, core, layer = transposed(
        f_low, d_low, x_mid, x_root, s_root, column_after, core, layer
    )
    x_low = s_low.astype(BF16)

    y_own = jnp.concatenate([x_root, x_mid, x_low], axis=1)
    before, after = neighbours(y_own)
    others = swap(jnp.concatenate([part[:, w_root:] for part in (before, y_own, after)], axis=1))
    window = jnp.concatenate([before, y_own, after, others], axis=1)
    my_part = mass_partial(window, column_after, mass_vals).astype(BF16)

    other = others[:, w_own : 2 * w_own]
    own = y_own[:, w_root:]
    first = jnp.where(core == 0, own, other)
    second = jnp.where(core == 0, other, own)
    y_all = jnp.concatenate(
        [x_root, first[:, :w_mid], second[:, :w_mid], first[:, w_mid:], second[:, w_mid:]], axis=1
    )

    mass_part = jnp.einsum("jr,kr->jk", y_all, my_part, preferred_element_type=F32)
    size = modes // layers
    y_mine = lax.dynamic_slice_in_dim(y_own, layer * size, size, axis=0)
    rows = lax.broadcasted_iota(jnp.int32, y_mine.shape, 1)
    y_mine = jnp.where((core == 0) | (rows >= w_root), y_mine, 0).astype(BF16)
    stiff_part = jnp.einsum("jr,kr->jk", y_mine, z, preferred_element_type=F32)

    def paired(value):
        size = value.shape[0] // 2
        return jnp.concatenate([value[:size], value[size:]], axis=1)

    n_mass, n_stiff = modes // 2, size // 2
    grams = jnp.concatenate([paired(mass_part), paired(stiff_part)], axis=0)
    grams = jnp.pad(grams, ((0, -(n_mass + n_stiff) % 8), (0, 0)))
    grams, y_all, s_root = full_sum(grams, "subtree", y_all, s_root)
    (grams,) = gather(grams.astype(BF16), FRONT)
    mass = total(grams[:, :n_mass])
    stiff = grams[:, n_mass : n_mass + n_stiff].astype(F32)
    stiff = jnp.sum(stiff.reshape(layers, 2, n_stiff, 2, modes), axis=1)
    stiff = jnp.transpose(stiff, (0, 2, 1, 3)).reshape(modes, modes)
    mass = jnp.concatenate([mass[:, :modes], mass[:, modes:]], axis=0)

    def output(flat, count):
        return jnp.transpose(flat.reshape(modes, count, -1), (1, 0, 2)).astype(F32)

    low_from = w_root + 2 * w_mid
    return (
        s_root[None],
        output(y_all[:, w_root:low_from], 2),
        output(y_all[:, low_from:], 4),
        stiff,
        mass,
    )


def solution(mesh):
    owners, fronts = mesh.shape["subtree"], mesh.shape["front"]
    split = Mesh(mesh.devices.reshape(owners, fronts // 2, 2), ("subtree", *FRONT))
    factor = P(None, FRONT, "subtree")
    update = P(None, "subtree", FRONT)
    rows = P(None, None, "subtree")
    return jax.shard_map(
        per_device,
        mesh=split,
        in_specs=(
            rows,
            rows,
            rows,
            factor,
            factor,
            factor,
            update,
            update,
            P(None, "subtree"),
            P(None, "subtree"),
            P("subtree", FRONT, None, None),
            P("subtree", FRONT),
        ),
        out_specs=(rows, rows, rows, P(), P()),
        check_vma=False,
    )
```

```python
import functools

import jax
import jax.numpy as jnp
from jax import lax
from jax.experimental import pallas as pl
from jax.experimental.pallas import tpu as pltpu
from jax.sharding import Mesh, PartitionSpec as P


BLOCK = 128
F32 = jnp.float32
BF16 = jnp.bfloat16
FRONT = ("z", "core")


def total(parts):
    return jnp.sum(parts.astype(F32), axis=0)


def exchange(pieces, axis, held):
    return lax.optimization_barrier((lax.all_to_all(pieces, axis, 0, 0), *held))


def gather(piece, axis, *held):
    copies = jnp.broadcast_to(piece[None], (lax.axis_size(axis), *piece.shape))
    return exchange(copies, axis, held)


def scatter_sum(pieces, axis, *held):
    got, *held = exchange(pieces.astype(BF16), axis, held)
    return total(got), *held


def full_sum(part, axis, *held):
    got, *held = gather(part.astype(BF16), axis, *held)
    return total(got), *held


def swap(value):
    return lax.ppermute(value, "core", [(0, 1), (1, 0)])


def neighbours(flat):
    count = lax.axis_size("subtree")
    before = lax.ppermute(flat, "subtree", [(i, i + 1) for i in range(count - 1)])
    after = lax.ppermute(flat, "subtree", [(i + 1, i) for i in range(count - 1)])
    return before, after


def _lanes(width):
    return [slice(at, at + 256) for at in range(0, width, 256)]


def _run(moves, sems):
    copies = [pltpu.make_async_copy(*move, sems.at[i]) for i, move in enumerate(moves)]
    for copy in copies:
        copy.start()
    for copy in copies:
        copy.wait()


def _pack_kernel(core_ref, *refs, count):
    weights, sent, stacks = refs[:count], refs[count], refs[count + 1 : 2 * count + 1]
    staged, halves, sems = refs[2 * count + 1], refs[2 * count + 2 : -1], refs[-1]
    core = core_ref[0]
    moves = []
    row = 0
    for weight, half in zip(weights, halves):
        nodes, rows, width = half.shape
        moves.append((weight.at[pl.ds(core * nodes, nodes)], half))
        for node in range(nodes):
            for lanes in _lanes(width):
                source = weight.at[(1 - core) * nodes + node, :, lanes]
                moves.append((source, staged.at[row : row + rows]))
                row += rows
    _run(moves, sems)
    out = [(half, stack.at[0]) for half, stack in zip(halves, stacks)]
    _run([(staged, sent), *out], sems)


def _unpack_kernel(received, *refs, count):
    stacks, sems = refs[count : 2 * count], refs[-1]
    moves = []
    row = 0
    for stack in stacks:
        nodes, rows, width = stack.shape[1:]
        for node in range(nodes):
            for lanes in _lanes(width):
                moves.append((received.at[row : row + rows], stack.at[1, node, :, lanes]))
                row += rows
    _run(moves, sems)


def _side_by_side_kernel(*refs):
    levels, flat, sems = refs[:-2], refs[-2], refs[-1]
    moves = []
    at = 0
    for level in levels:
        nodes, _, width = level.shape
        for node in range(nodes):
            moves.append((level.at[node], flat.at[:, at : at + width]))
            at += width
    _run(moves, sems)


def side_by_side(*levels):
    width = sum(level.shape[0] * level.shape[2] for level in levels)
    return pl.pallas_call(
        _side_by_side_kernel,
        out_shape=jax.ShapeDtypeStruct((levels[0].shape[1], width), BF16),
        in_specs=[pl.BlockSpec(memory_space=pl.ANY)] * len(levels),
        out_specs=pl.BlockSpec(memory_space=pltpu.VMEM),
        scratch_shapes=[pltpu.SemaphoreType.DMA((sum(level.shape[0] for level in levels),))],
        name="side_by_side",
    )(*levels)


def split_nodes(core, *weights):
    count = len(weights)
    shapes = [(2, w.shape[0] // 2, *w.shape[1:]) for w in weights]
    crossing = sum(n * (width // 256) for _, n, _, width in shapes)
    rows = sum(n * r * (width // 256) for _, n, r, width in shapes)
    anywhere = pl.BlockSpec(memory_space=pl.ANY)
    sent, *stacks = pl.pallas_call(
        functools.partial(_pack_kernel, count=count),
        out_shape=[jax.ShapeDtypeStruct(shape, BF16) for shape in ((rows, 256), *shapes)],
        in_specs=[pl.BlockSpec(memory_space=pltpu.SMEM)] + [anywhere] * count,
        out_specs=[anywhere] * (count + 1),
        scratch_shapes=[
            pltpu.VMEM((rows, 256), BF16),
            *(pltpu.VMEM(shape[1:], BF16) for shape in shapes),
            pltpu.SemaphoreType.DMA((crossing + count,)),
        ],
        name="pack",
    )(core.reshape(1), *weights)
    return stacks, swap(sent)


def unpacked(stacks, received):
    count = len(stacks)
    crossing = sum(s.shape[1] * (s.shape[3] // 256) for s in stacks)
    anywhere = pl.BlockSpec(memory_space=pl.ANY)
    return pl.pallas_call(
        functools.partial(_unpack_kernel, count=count),
        out_shape=[jax.ShapeDtypeStruct(s.shape, BF16) for s in stacks],
        in_specs=[pl.BlockSpec(memory_space=pltpu.VMEM)] + [anywhere] * count,
        out_specs=[anywhere] * count,
        input_output_aliases={i + 1: i for i in range(count)},
        scratch_shapes=[pltpu.SemaphoreType.DMA((crossing,))],
        name="unpack",
    )(pltpu.with_memory_space_constraint(received, pltpu.VMEM), *stacks)


def to_pieces(value, count, width):
    lead = value.size // value.shape[-1] // 8
    blocks = value.reshape(lead, 8, -1, width).transpose(0, 2, 1, 3).reshape(-1, 8, width)
    spare = count - blocks.shape[0]
    if spare:
        blocks = jnp.concatenate([blocks, jnp.zeros((spare, 8, width), blocks.dtype)], axis=0)
    return blocks


def from_pieces(blocks, shape):
    width = blocks.shape[-1]
    across = shape[-1] // width
    lead = 1
    for size in shape[:-1]:
        lead *= size
    used = blocks[: lead // 8 * across]
    return used.reshape(lead // 8, across, 8, width).transpose(0, 2, 1, 3).reshape(shape)


def mass_partial(window, column, mass_vals):
    modes = window.shape[0]
    picked = window.reshape(modes, -1, BLOCK)[:, column, :]
    product = jnp.einsum("mrei,reoi->mro", picked, mass_vals, preferred_element_type=F32)
    return product.reshape(modes, -1)


def _unpaired_kernel(grams, stiff, mass, *, n_mass, n_stiff):
    modes = mass.shape[1]
    every = jnp.sum(grams[:, :n_mass, :].astype(F32), axis=0)
    mass[:n_mass] = every[:, :modes]
    mass[n_mass:] = every[:, modes:]
    for layer in range(grams.shape[0] // 2):
        rows = slice(n_mass, n_mass + 8)
        pair = grams[2 * layer, rows, :].astype(F32) + grams[2 * layer + 1, rows, :].astype(F32)
        at = 2 * n_stiff * layer
        stiff[at : at + n_stiff] = pair[:n_stiff, :modes]
        stiff[at + n_stiff : at + 2 * n_stiff] = pair[:n_stiff, modes:]


def unpaired(grams, n_mass, n_stiff):
    modes = grams.shape[2] // 2
    return pl.pallas_call(
        functools.partial(_unpaired_kernel, n_mass=n_mass, n_stiff=n_stiff),
        out_shape=[jax.ShapeDtypeStruct((modes, modes), F32)] * 2,
        in_specs=[pl.BlockSpec(memory_space=pltpu.VMEM)],
        name="unpaired",
    )(pltpu.with_memory_space_constraint(grams, pltpu.VMEM))


def per_device(
    modes_root,
    modes_mid,
    modes_low,
    factor_root,
    factor_mid,
    factor_low,
    update_mid,
    update_low,
    map_mid,
    map_low,
    mass_vals,
    mass_cols,
):
    owner = lax.axis_index("subtree")
    core = lax.axis_index("core")
    owners = lax.axis_size("subtree")
    layers = lax.axis_size("z")
    modes = modes_root.shape[1]
    w_root, w_mid, w_low = modes_root.shape[2], modes_mid.shape[2], modes_low.shape[2]
    b_root, b_mid, b_low = w_root // BLOCK, w_mid // BLOCK, w_low // BLOCK
    local_blocks = b_root + 2 * b_mid + 4 * b_low
    b_own = b_mid + 2 * b_low
    w_own = b_own * BLOCK
    mid_at, low_at = w_root, w_root + w_mid

    def half(value, which, axis=0):
        size = value.shape[axis] // 2
        return lax.dynamic_slice_in_dim(value, which * size, size, axis)

    column = mass_cols - (owner - 1) * local_blocks
    place = column // local_blocks
    block = column % local_blocks
    is_low = block >= b_root + 2 * b_mid
    after_root = block - b_root
    low_block = after_root - 2 * b_mid
    of = jnp.where(is_low, low_block // (2 * b_low), after_root // b_mid)
    within = jnp.where(is_low, b_mid + low_block % (2 * b_low), after_root % b_mid)
    b_window = b_root + b_own
    mine = jnp.where(block < b_root, block, b_root + within) + place * b_window
    theirs = 3 * b_window + place * b_own + within
    column_after = jnp.where((block < b_root) | (of == core), mine, theirs)
    t_mid = half(map_mid, core)[:, 0] - owner * local_blocks
    t_low = half(map_low, core)[:, 0] - owner * local_blocks
    first_mid = b_root + core * b_mid

    def forward(stack, right, *held):
        part = jnp.einsum("hnij,mnj->hnmi", stack, right, preferred_element_type=F32)
        width = part.size // owners // 8
        return scatter_sum(to_pieces(part.astype(BF16), owners, width), "subtree", *held)

    def whole(piece, shape, *held):
        got, *held = gather(piece.astype(BF16), "subtree", *held)
        return from_pieces(got, shape), *held

    def update_term(stack, y, *held):
        part = jnp.einsum("hnai,hnmi->nma", stack, y, preferred_element_type=F32)
        return full_sum(part, "z", *held)

    def placed(term, target, count):
        blocks = []
        for index in range(count):
            hit = (target == index)[:, None, None]
            blocks.append(jnp.sum(jnp.where(hit, term, 0.0), axis=0))
        return jnp.concatenate(blocks, axis=1)

    def back_term(stack, candidates, *held):
        g = jnp.zeros((stack.shape[1], modes, BLOCK), BF16)
        for hit, block in candidates:
            g = jnp.where(hit[:, None, None], block[None], g)
        part = jnp.einsum("hnai,nma->hnmi", stack, g, preferred_element_type=F32)
        width = part.size // owners // 8
        return scatter_sum(to_pieces(part.astype(BF16), owners, width), "subtree", *held)

    def transposed(stack, d, *held):
        part = jnp.einsum("hnij,hnmi->nmj", stack, d, preferred_element_type=F32)
        return full_sum(jnp.transpose(part, (1, 0, 2)).reshape(modes, -1), "z", *held)

    def cut(flat, target, count):
        return [(target == i, flat[:, i * BLOCK : (i + 1) * BLOCK]) for i in range(count)]

    stacked = side_by_side(modes_root, modes_mid, modes_low)
    before, after = neighbours(stacked)
    window = jnp.concatenate([before, stacked, after], axis=1)
    z_part = mass_partial(window, column, mass_vals).astype(BF16)

    def of_core(flat, which):
        mid = w_root + which * w_mid
        low = w_root + 2 * w_mid + which * 2 * w_low
        return jnp.concatenate(
            [flat[:, :w_root], flat[:, mid : mid + w_mid], flat[:, low : low + 2 * w_low]], axis=1
        )

    z_part = jnp.stack([of_core(z_part, 0), of_core(z_part, 1)]).reshape(
        2, layers, modes // layers, w_root + w_own
    )
    z_part = jnp.transpose(z_part, (1, 0, 2, 3)).reshape(2 * layers, *z_part.shape[2:])
    layer = lax.axis_index("z")
    t_own = t_low - first_mid
    z_part, t_mid, t_low, t_own, column_after, core, layer = lax.optimization_barrier(
        (z_part, t_mid, t_low, t_own, column_after, core, layer)
    )
    stacks, received = split_nodes(core, factor_low, factor_mid, update_low, update_mid)
    (z_mine,) = scatter_sum(z_part, FRONT)
    f_low, f_mid, u_low, u_mid = unpacked(stacks, received)
    (z,) = gather(z_mine.astype(BF16), "z")
    z = z.reshape(modes, -1)

    right = z[:, low_at:].reshape(modes, 2, w_low)
    y_low, t_low, t_own = forward(f_low, right, t_low, t_own)
    y, t_low, t_own = whole(y_low, (2, 2, modes, f_low.shape[-2]), t_low, t_own)
    term, t_low, t_own = update_term(u_low, y, t_low, t_own)
    acc_mid = placed(term, t_own, b_mid)
    acc_root = placed(term, t_low, b_root)
    right = (z[:, mid_at:low_at].astype(F32) - acc_mid).astype(BF16)
    right, acc_root = lax.optimization_barrier((right, acc_root))
    y_mid, t_mid = forward(f_mid, right.reshape(modes, 1, w_mid), t_mid)
    y, t_mid = whole(y_mid, (2, 1, modes, f_mid.shape[-2]), t_mid)
    term, t_mid, acc_root = update_term(u_mid, y, t_mid, acc_root)
    acc_root = acc_root + placed(term, t_mid, b_root)
    acc_root = acc_root + swap(acc_root)
    right = (z[:, :mid_at].astype(F32) - acc_root).astype(BF16)
    part = jnp.einsum("ij,mj->mi", factor_root[0], right, preferred_element_type=F32)
    (y_root,) = scatter_sum(to_pieces(part.astype(BF16), owners, 2 * BLOCK), "subtree")

    (d_root,) = whole(y_root, part.shape)
    part = jnp.einsum("ij,mi->mj", factor_root[0], d_root, preferred_element_type=F32)
    s_root, t_mid = full_sum(part + swap(part), "z", t_mid)
    x_root = s_root.astype(BF16)
    root_blocks = cut(x_root, t_mid, b_root)
    v_mid, y_mid, x_root = back_term(u_mid, root_blocks, y_mid, x_root)
    d_mid, x_root = whole(y_mid - v_mid, (2, 1, modes, f_mid.shape[-2]), x_root)
    s_mid, x_root, t_low, t_own = transposed(f_mid, d_mid, x_root, t_low, t_own)
    x_mid = s_mid.astype(BF16)
    blocks = cut(x_root, t_low, b_root) + cut(x_mid, t_own, b_mid)
    v_low, y_low, x_mid, x_root = back_term(u_low, blocks, y_low, x_mid, x_root)
    d_low, x_mid, x_root = whole(y_low - v_low, (2, 2, modes, f_low.shape[-2]), x_mid, x_root)
    s_low, x_mid, x_root, s_root, column_after, core, layer = transposed(
        f_low, d_low, x_mid, x_root, s_root, column_after, core, layer
    )
    x_low = s_low.astype(BF16)

    y_own = jnp.concatenate([x_root, x_mid, x_low], axis=1)
    before, after = neighbours(y_own)
    others = swap(jnp.concatenate([part[:, w_root:] for part in (before, y_own, after)], axis=1))
    window = jnp.concatenate([before, y_own, after, others], axis=1)
    my_part = mass_partial(window, column_after, mass_vals).astype(BF16)

    other = others[:, w_own : 2 * w_own]
    own = y_own[:, w_root:]
    first = jnp.where(core == 0, own, other)
    second = jnp.where(core == 0, other, own)
    y_all = jnp.concatenate(
        [x_root, first[:, :w_mid], second[:, :w_mid], first[:, w_mid:], second[:, w_mid:]], axis=1
    )

    mass_part = jnp.einsum("jr,kr->jk", y_all, my_part, preferred_element_type=F32)
    size = modes // layers
    y_mine = lax.dynamic_slice_in_dim(y_own, layer * size, size, axis=0)
    rows = lax.broadcasted_iota(jnp.int32, y_mine.shape, 1)
    y_mine = jnp.where((core == 0) | (rows >= w_root), y_mine, 0).astype(BF16)
    stiff_part = jnp.einsum("jr,kr->jk", y_mine, z, preferred_element_type=F32)

    def paired(value):
        size = value.shape[0] // 2
        return jnp.concatenate([value[:size], value[size:]], axis=1)

    n_mass, n_stiff = modes // 2, size // 2
    grams = jnp.concatenate([paired(mass_part), paired(stiff_part)], axis=0)
    grams = jnp.pad(grams, ((0, -(n_mass + n_stiff) % 8), (0, 0)))
    grams, y_all, s_root = full_sum(grams, "subtree", y_all, s_root)
    (grams,) = gather(grams.astype(BF16), FRONT)
    stiff, mass = unpaired(grams, n_mass, n_stiff)

    def output(flat, count):
        return jnp.transpose(flat.reshape(modes, count, -1), (1, 0, 2)).astype(F32)

    low_from = w_root + 2 * w_mid
    return (
        s_root[None],
        output(y_all[:, w_root:low_from], 2),
        output(y_all[:, low_from:], 4),
        stiff,
        mass,
    )


def solution(mesh):
    owners, fronts = mesh.shape["subtree"], mesh.shape["front"]
    split = Mesh(mesh.devices.reshape(owners, fronts // 2, 2), ("subtree", *FRONT))
    factor = P(None, FRONT, "subtree")
    update = P(None, "subtree", FRONT)
    rows = P(None, None, "subtree")

    return jax.shard_map(
        per_device,
        mesh=split,
        in_specs=(
            rows,
            rows,
            rows,
            factor,
            factor,
            factor,
            update,
            update,
            P(None, "subtree"),
            P(None, "subtree"),
            P("subtree", FRONT, None, None),
            P("subtree", FRONT),
        ),
        out_specs=(rows, rows, rows, P(), P()),
        check_vma=False,
    )
```

```python
import functools

import jax
import jax.numpy as jnp
from jax import lax
from jax.experimental import pallas as pl
from jax.experimental.pallas import tpu as pltpu
from jax.sharding import Mesh, PartitionSpec as P


BLOCK = 128
F32 = jnp.float32
BF16 = jnp.bfloat16
FRONT = ("z", "core")


def total(parts):
    return jnp.sum(parts.astype(F32), axis=0)


def exchange(pieces, axis, held):
    return lax.optimization_barrier((lax.all_to_all(pieces, axis, 0, 0), *held))


def gather(piece, axis, *held):
    copies = jnp.broadcast_to(piece[None], (lax.axis_size(axis), *piece.shape))
    return exchange(copies, axis, held)


def scatter_sum(pieces, axis, *held):
    got, *held = exchange(pieces.astype(BF16), axis, held)
    return total(got), *held


def full_sum(part, axis, *held):
    got, *held = gather(part.astype(BF16), axis, *held)
    return total(got), *held


def swap(value):
    return lax.ppermute(value, "core", [(0, 1), (1, 0)])


def neighbours(flat):
    count = lax.axis_size("subtree")
    before = lax.ppermute(flat, "subtree", [(i, i + 1) for i in range(count - 1)])
    after = lax.ppermute(flat, "subtree", [(i + 1, i) for i in range(count - 1)])
    return before, after


def _lanes(width):
    return [slice(at, at + 256) for at in range(0, width, 256)]


def _run(moves, sems):
    copies = [pltpu.make_async_copy(*move, sems.at[i]) for i, move in enumerate(moves)]
    for copy in copies:
        copy.start()
    for copy in copies:
        copy.wait()


def _pack_kernel(core_ref, *refs, count):
    weights, sent, stacks = refs[:count], refs[count], refs[count + 1 : 2 * count + 1]
    staged, halves, sems = refs[2 * count + 1], refs[2 * count + 2 : -1], refs[-1]
    core = core_ref[0]
    moves = []
    row = 0
    for weight, half in zip(weights, halves):
        nodes, rows, width = half.shape
        moves.append((weight.at[pl.ds(core * nodes, nodes)], half))
        for node in range(nodes):
            for lanes in _lanes(width):
                source = weight.at[(1 - core) * nodes + node, :, lanes]
                moves.append((source, staged.at[row : row + rows]))
                row += rows
    _run(moves, sems)
    out = [(half, stack.at[0]) for half, stack in zip(halves, stacks)]
    _run([(staged, sent), *out], sems)


def _unpack_kernel(received, *refs, count):
    stacks, sems = refs[count : 2 * count], refs[-1]
    moves = []
    row = 0
    for stack in stacks:
        nodes, rows, width = stack.shape[1:]
        for node in range(nodes):
            for lanes in _lanes(width):
                moves.append((received.at[row : row + rows], stack.at[1, node, :, lanes]))
                row += rows
    _run(moves, sems)


def _side_by_side_kernel(*refs):
    levels, flat, sems = refs[:-2], refs[-2], refs[-1]
    moves = []
    at = 0
    for level in levels:
        nodes, _, width = level.shape
        for node in range(nodes):
            moves.append((level.at[node], flat.at[:, at : at + width]))
            at += width
    _run(moves, sems)


def side_by_side(*levels):
    width = sum(level.shape[0] * level.shape[2] for level in levels)
    return pl.pallas_call(
        _side_by_side_kernel,
        out_shape=jax.ShapeDtypeStruct((levels[0].shape[1], width), BF16),
        in_specs=[pl.BlockSpec(memory_space=pl.ANY)] * len(levels),
        out_specs=pl.BlockSpec(memory_space=pltpu.VMEM),
        scratch_shapes=[pltpu.SemaphoreType.DMA((sum(level.shape[0] for level in levels),))],
        name="side_by_side",
    )(*levels)


def split_nodes(core, *weights):
    count = len(weights)
    shapes = [(2, w.shape[0] // 2, *w.shape[1:]) for w in weights]
    crossing = sum(n * (width // 256) for _, n, _, width in shapes)
    rows = sum(n * r * (width // 256) for _, n, r, width in shapes)
    anywhere = pl.BlockSpec(memory_space=pl.ANY)
    sent, *stacks = pl.pallas_call(
        functools.partial(_pack_kernel, count=count),
        out_shape=[jax.ShapeDtypeStruct(shape, BF16) for shape in ((rows, 256), *shapes)],
        in_specs=[pl.BlockSpec(memory_space=pltpu.SMEM)] + [anywhere] * count,
        out_specs=[anywhere] * (count + 1),
        scratch_shapes=[
            pltpu.VMEM((rows, 256), BF16),
            *(pltpu.VMEM(shape[1:], BF16) for shape in shapes),
            pltpu.SemaphoreType.DMA((crossing + count,)),
        ],
        name="pack",
    )(core.reshape(1), *weights)
    return stacks, swap(sent)


def unpacked(stacks, received):
    count = len(stacks)
    crossing = sum(s.shape[1] * (s.shape[3] // 256) for s in stacks)
    anywhere = pl.BlockSpec(memory_space=pl.ANY)
    return pl.pallas_call(
        functools.partial(_unpack_kernel, count=count),
        out_shape=[jax.ShapeDtypeStruct(s.shape, BF16) for s in stacks],
        in_specs=[pl.BlockSpec(memory_space=pltpu.VMEM)] + [anywhere] * count,
        out_specs=[anywhere] * count,
        input_output_aliases={i + 1: i for i in range(count)},
        scratch_shapes=[pltpu.SemaphoreType.DMA((crossing,))],
        name="unpack",
    )(pltpu.with_memory_space_constraint(received, pltpu.VMEM), *stacks)


def to_pieces(value, count, width):
    lead = value.size // value.shape[-1] // 8
    blocks = value.reshape(lead, 8, -1, width).transpose(0, 2, 1, 3).reshape(-1, 8, width)
    spare = count - blocks.shape[0]
    if spare:
        blocks = jnp.concatenate([blocks, jnp.zeros((spare, 8, width), blocks.dtype)], axis=0)
    return blocks


def from_pieces(blocks, shape):
    width = blocks.shape[-1]
    across = shape[-1] // width
    lead = 1
    for size in shape[:-1]:
        lead *= size
    used = blocks[: lead // 8 * across]
    return used.reshape(lead // 8, across, 8, width).transpose(0, 2, 1, 3).reshape(shape)


def mass_partial(window, column, mass_vals):
    modes = window.shape[0]
    picked = window.reshape(modes, -1, BLOCK)[:, column, :]
    product = jnp.einsum("mrei,reoi->mro", picked, mass_vals, preferred_element_type=F32)
    return product.reshape(modes, -1)


def _unpaired_kernel(grams, stiff, mass, *, n_mass, n_stiff):
    modes = mass.shape[1]
    every = jnp.sum(grams[:, :n_mass, :].astype(F32), axis=0)
    mass[:n_mass] = every[:, :modes]
    mass[n_mass:] = every[:, modes:]
    for layer in range(grams.shape[0] // 2):
        rows = slice(n_mass, n_mass + 8)
        pair = grams[2 * layer, rows, :].astype(F32) + grams[2 * layer + 1, rows, :].astype(F32)
        at = 2 * n_stiff * layer
        stiff[at : at + n_stiff] = pair[:n_stiff, :modes]
        stiff[at + n_stiff : at + 2 * n_stiff] = pair[:n_stiff, modes:]


def unpaired(grams, n_mass, n_stiff):
    modes = grams.shape[2] // 2
    return pl.pallas_call(
        functools.partial(_unpaired_kernel, n_mass=n_mass, n_stiff=n_stiff),
        out_shape=[jax.ShapeDtypeStruct((modes, modes), F32)] * 2,
        in_specs=[pl.BlockSpec(memory_space=pltpu.VMEM)],
        name="unpaired",
    )(pltpu.with_memory_space_constraint(grams, pltpu.VMEM))


def per_device(
    modes_root,
    modes_mid,
    modes_low,
    factor_root,
    factor_mid,
    factor_low,
    update_mid,
    update_low,
    map_mid,
    map_low,
    mass_vals,
    mass_cols,
):
    owner = lax.axis_index("subtree")
    core = lax.axis_index("core")
    owners = lax.axis_size("subtree")
    layers = lax.axis_size("z")
    modes = modes_root.shape[1]
    w_root, w_mid, w_low = modes_root.shape[2], modes_mid.shape[2], modes_low.shape[2]
    b_root, b_mid, b_low = w_root // BLOCK, w_mid // BLOCK, w_low // BLOCK
    local_blocks = b_root + 2 * b_mid + 4 * b_low
    b_own = b_mid + 2 * b_low
    w_own = b_own * BLOCK
    mid_at, low_at = w_root, w_root + w_mid

    def half(value, which, axis=0):
        size = value.shape[axis] // 2
        return lax.dynamic_slice_in_dim(value, which * size, size, axis)

    column = mass_cols - (owner - 1) * local_blocks
    place = column // local_blocks
    block = column % local_blocks
    is_low = block >= b_root + 2 * b_mid
    after_root = block - b_root
    low_block = after_root - 2 * b_mid
    of = jnp.where(is_low, low_block // (2 * b_low), after_root // b_mid)
    within = jnp.where(is_low, b_mid + low_block % (2 * b_low), after_root % b_mid)
    b_window = b_root + b_own
    mine = jnp.where(block < b_root, block, b_root + within) + place * b_window
    theirs = 3 * b_window + place * b_own + within
    column_after = jnp.where((block < b_root) | (of == core), mine, theirs)
    t_mid = half(map_mid, core)[:, 0] - owner * local_blocks
    t_low = half(map_low, core)[:, 0] - owner * local_blocks
    first_mid = b_root + core * b_mid

    def forward(stack, right, *held):
        part = jnp.einsum("hnij,mnj->hnmi", stack, right, preferred_element_type=F32)
        width = part.size // owners // 8
        return scatter_sum(to_pieces(part.astype(BF16), owners, width), "subtree", *held)

    def whole(piece, shape, *held):
        got, *held = gather(piece.astype(BF16), "subtree", *held)
        return from_pieces(got, shape), *held

    def update_term(stack, y, *held):
        part = jnp.einsum("hnai,hnmi->nma", stack, y, preferred_element_type=F32)
        return full_sum(part, "z", *held)

    def placed(term, target, count):
        blocks = []
        for index in range(count):
            hit = (target == index)[:, None, None]
            blocks.append(jnp.sum(jnp.where(hit, term, 0.0), axis=0))
        return jnp.concatenate(blocks, axis=1)

    def back_term(stack, candidates, *held):
        g = jnp.zeros((stack.shape[1], modes, BLOCK), BF16)
        for hit, block in candidates:
            g = jnp.where(hit[:, None, None], block[None], g)
        part = jnp.einsum("hnai,nma->hnmi", stack, g, preferred_element_type=F32)
        width = part.size // owners // 8
        return scatter_sum(to_pieces(part.astype(BF16), owners, width), "subtree", *held)

    def transposed(stack, d, *held):
        part = jnp.einsum("hnij,hnmi->nmj", stack, d, preferred_element_type=F32)
        return full_sum(jnp.transpose(part, (1, 0, 2)).reshape(modes, -1), "z", *held)

    def cut(flat, target, count):
        return [(target == i, flat[:, i * BLOCK : (i + 1) * BLOCK]) for i in range(count)]

    stacked = side_by_side(modes_root, modes_mid, modes_low)
    before, after = neighbours(stacked)
    factors_root = (factor_root[0], swap(factor_root[0]))
    window = jnp.concatenate([before, stacked, after], axis=1)
    z_part = mass_partial(window, column, mass_vals).astype(BF16)

    def of_core(flat, which):
        mid = w_root + which * w_mid
        low = w_root + 2 * w_mid + which * 2 * w_low
        return jnp.concatenate(
            [flat[:, :w_root], flat[:, mid : mid + w_mid], flat[:, low : low + 2 * w_low]], axis=1
        )

    z_part = jnp.stack([of_core(z_part, 0), of_core(z_part, 1)]).reshape(
        2, layers, modes // layers, w_root + w_own
    )
    z_part = jnp.transpose(z_part, (1, 0, 2, 3)).reshape(2 * layers, *z_part.shape[2:])
    layer = lax.axis_index("z")
    t_own = t_low - first_mid
    z_part, t_mid, t_low, t_own, column_after, core, layer = lax.optimization_barrier(
        (z_part, t_mid, t_low, t_own, column_after, core, layer)
    )
    stacks, received = split_nodes(core, factor_low, factor_mid, update_low, update_mid)
    (z_mine,) = scatter_sum(z_part, FRONT)
    f_low, f_mid, u_low, u_mid = unpacked(stacks, received)
    (z,) = gather(z_mine.astype(BF16), "z")
    z = z.reshape(modes, -1)

    right = z[:, low_at:].reshape(modes, 2, w_low)
    y_low, t_low, t_own = forward(f_low, right, t_low, t_own)
    y, t_low, t_own = whole(y_low, (2, 2, modes, f_low.shape[-2]), t_low, t_own)
    term, t_low, t_own = update_term(u_low, y, t_low, t_own)
    acc_mid = placed(term, t_own, b_mid)
    acc_root = placed(term, t_low, b_root)
    right = (z[:, mid_at:low_at].astype(F32) - acc_mid).astype(BF16)
    right, acc_root = lax.optimization_barrier((right, acc_root))
    y_mid, t_mid = forward(f_mid, right.reshape(modes, 1, w_mid), t_mid)
    y, t_mid = whole(y_mid, (2, 1, modes, f_mid.shape[-2]), t_mid)
    term, t_mid, acc_root = update_term(u_mid, y, t_mid, acc_root)
    acc_root = acc_root + placed(term, t_mid, b_root)

    half_modes = modes // 2
    z_root, t_mid, core = lax.optimization_barrier((z[:, :mid_at], t_mid, core))

    def of_modes(value, which):
        return lax.dynamic_slice_in_dim(value, which * half_modes, half_modes, 0)

    acc_root = of_modes(acc_root, core) + swap(of_modes(acc_root, 1 - core))
    right = (of_modes(z_root, core).astype(F32) - acc_root).astype(BF16)

    def by_core(mine, other):
        return jnp.concatenate(
            [jnp.where(core == 0, mine, other), jnp.where(core == 0, other, mine)], axis=0
        )

    part = jnp.stack(
        [jnp.einsum("ij,mj->mi", f, right, preferred_element_type=F32) for f in factors_root]
    )
    (y_root,) = scatter_sum(to_pieces(part.astype(BF16), owners, 2 * BLOCK), "subtree")

    d_root, t_mid, core = whole(y_root, part.shape, t_mid, core)
    part = sum(
        jnp.einsum("ij,mi->mj", f, d, preferred_element_type=F32)
        for f, d in zip(factors_root, d_root)
    )
    s_half, t_mid, core = full_sum(part, "z", t_mid, core)
    s_other = swap(s_half)
    x_root = by_core(s_half.astype(BF16), s_other.astype(BF16))
    x_root = lax.optimization_barrier(x_root)
    root_blocks = cut(x_root, t_mid, b_root)
    v_mid, y_mid, x_root = back_term(u_mid, root_blocks, y_mid, x_root)
    d_mid, x_root = whole(y_mid - v_mid, (2, 1, modes, f_mid.shape[-2]), x_root)
    s_mid, x_root, t_low, t_own = transposed(f_mid, d_mid, x_root, t_low, t_own)
    x_mid = s_mid.astype(BF16)
    blocks = cut(x_root, t_low, b_root) + cut(x_mid, t_own, b_mid)
    v_low, y_low, x_mid, x_root = back_term(u_low, blocks, y_low, x_mid, x_root)
    d_low, x_mid, x_root = whole(y_low - v_low, (2, 2, modes, f_low.shape[-2]), x_mid, x_root)
    s_low, x_mid, x_root, s_half, s_other, column_after, core, layer = transposed(
        f_low, d_low, x_mid, x_root, s_half, s_other, column_after, core, layer
    )
    x_low = s_low.astype(BF16)

    y_own = jnp.concatenate([x_root, x_mid, x_low], axis=1)
    before, after = neighbours(y_own)
    others = swap(jnp.concatenate([part[:, w_root:] for part in (before, y_own, after)], axis=1))
    window = jnp.concatenate([before, y_own, after, others], axis=1)
    my_part = mass_partial(window, column_after, mass_vals).astype(BF16)

    other = others[:, w_own : 2 * w_own]
    own = y_own[:, w_root:]
    first = jnp.where(core == 0, own, other)
    second = jnp.where(core == 0, other, own)
    y_all = jnp.concatenate(
        [x_root, first[:, :w_mid], second[:, :w_mid], first[:, w_mid:], second[:, w_mid:]], axis=1
    )

    mass_part = jnp.einsum("jr,kr->jk", y_all, my_part, preferred_element_type=F32)
    size = modes // layers
    y_mine = lax.dynamic_slice_in_dim(y_own, layer * size, size, axis=0)
    rows = lax.broadcasted_iota(jnp.int32, y_mine.shape, 1)
    y_mine = jnp.where((core == 0) | (rows >= w_root), y_mine, 0).astype(BF16)
    stiff_part = jnp.einsum("jr,kr->jk", y_mine, z, preferred_element_type=F32)

    def paired(value):
        size = value.shape[0] // 2
        return jnp.concatenate([value[:size], value[size:]], axis=1)

    n_mass, n_stiff = modes // 2, size // 2
    grams = jnp.concatenate([paired(mass_part), paired(stiff_part)], axis=0)
    grams = jnp.pad(grams, ((0, -(n_mass + n_stiff) % 8), (0, 0)))
    grams, y_all, s_half, s_other = full_sum(grams, "subtree", y_all, s_half, s_other)
    (grams,) = gather(grams.astype(BF16), FRONT)
    stiff, mass = unpaired(grams, n_mass, n_stiff)

    def output(flat, count):
        return jnp.transpose(flat.reshape(modes, count, -1), (1, 0, 2)).astype(F32)

    low_from = w_root + 2 * w_mid
    solved_root = by_core(s_half, s_other)[None]
    solved_mid = output(y_all[:, w_root:low_from], 2)
    solved_low = output(y_all[:, low_from:], 4)
    return solved_root, solved_mid, solved_low, stiff, mass


def solution(mesh):
    owners, fronts = mesh.shape["subtree"], mesh.shape["front"]
    split = Mesh(mesh.devices.reshape(owners, fronts // 2, 2), ("subtree", *FRONT))
    factor = P(None, FRONT, "subtree")
    update = P(None, "subtree", FRONT)
    rows = P(None, None, "subtree")

    return jax.shard_map(
        per_device,
        mesh=split,
        in_specs=(
            rows,
            rows,
            rows,
            factor,
            factor,
            factor,
            update,
            update,
            P(None, "subtree"),
            P(None, "subtree"),
            P("subtree", FRONT, None, None),
            P("subtree", FRONT),
        ),
        out_specs=(rows, rows, rows, P(), P()),
        check_vma=False,
    )
```

```python
import functools

import jax
import jax.numpy as jnp
from jax import lax
from jax.experimental import pallas as pl
from jax.experimental.pallas import tpu as pltpu
from jax.sharding import Mesh, PartitionSpec as P


BLOCK = 128
F32 = jnp.float32
BF16 = jnp.bfloat16
FRONT = ("z", "core")


def total(parts):
    return jnp.sum(parts.astype(F32), axis=0)


def exchange(pieces, axis, held):
    return lax.optimization_barrier((lax.all_to_all(pieces, axis, 0, 0), *held))


def gather(piece, axis, *held):
    copies = jnp.broadcast_to(piece[None], (lax.axis_size(axis), *piece.shape))
    return exchange(copies, axis, held)


def scatter_sum(pieces, axis, *held):
    got, *held = exchange(pieces.astype(BF16), axis, held)
    return total(got), *held


def full_sum(part, axis, *held):
    got, *held = gather(part.astype(BF16), axis, *held)
    return total(got), *held


def swap(value):
    return lax.ppermute(value, "core", [(0, 1), (1, 0)])


def neighbours(flat):
    count = lax.axis_size("subtree")
    before = lax.ppermute(flat, "subtree", [(i, i + 1) for i in range(count - 1)])
    after = lax.ppermute(flat, "subtree", [(i + 1, i) for i in range(count - 1)])
    return before, after


def _lanes(width):
    return [slice(at, at + 256) for at in range(0, width, 256)]


def _run(moves, sems):
    copies = [pltpu.make_async_copy(*move, sems.at[i]) for i, move in enumerate(moves)]
    for copy in copies:
        copy.start()
    for copy in copies:
        copy.wait()


def _pack_kernel(core_ref, *refs, count):
    weights, sent, stacks = refs[:count], refs[count], refs[count + 1 : 2 * count + 1]
    staged, halves, sems = refs[2 * count + 1], refs[2 * count + 2 : -1], refs[-1]
    core = core_ref[0]
    moves = []
    row = 0
    for weight, half in zip(weights, halves):
        nodes, rows, width = half.shape
        moves.append((weight.at[pl.ds(core * nodes, nodes)], half))
        for node in range(nodes):
            for lanes in _lanes(width):
                source = weight.at[(1 - core) * nodes + node, :, lanes]
                moves.append((source, staged.at[row : row + rows]))
                row += rows
    _run(moves, sems)
    out = [(half, stack.at[0]) for half, stack in zip(halves, stacks)]
    _run([(staged, sent), *out], sems)


def _unpack_kernel(received, *refs, count):
    stacks, sems = refs[count : 2 * count], refs[-1]
    moves = []
    row = 0
    for stack in stacks:
        nodes, rows, width = stack.shape[1:]
        for node in range(nodes):
            for lanes in _lanes(width):
                moves.append((received.at[row : row + rows], stack.at[1, node, :, lanes]))
                row += rows
    _run(moves, sems)


def _side_by_side_kernel(*refs):
    levels, flat, sems = refs[:-2], refs[-2], refs[-1]
    moves = []
    at = 0
    for level in levels:
        nodes, _, width = level.shape
        for node in range(nodes):
            moves.append((level.at[node], flat.at[:, at : at + width]))
            at += width
    _run(moves, sems)


def side_by_side(*levels):
    width = sum(level.shape[0] * level.shape[2] for level in levels)
    return pl.pallas_call(
        _side_by_side_kernel,
        out_shape=jax.ShapeDtypeStruct((levels[0].shape[1], width), BF16),
        in_specs=[pl.BlockSpec(memory_space=pl.ANY)] * len(levels),
        out_specs=pl.BlockSpec(memory_space=pltpu.VMEM),
        scratch_shapes=[pltpu.SemaphoreType.DMA((sum(level.shape[0] for level in levels),))],
        name="side_by_side",
    )(*levels)


def split_nodes(core, *weights):
    count = len(weights)
    shapes = [(2, w.shape[0] // 2, *w.shape[1:]) for w in weights]
    crossing = sum(n * (width // 256) for _, n, _, width in shapes)
    rows = sum(n * r * (width // 256) for _, n, r, width in shapes)
    anywhere = pl.BlockSpec(memory_space=pl.ANY)
    sent, *stacks = pl.pallas_call(
        functools.partial(_pack_kernel, count=count),
        out_shape=[jax.ShapeDtypeStruct(shape, BF16) for shape in ((rows, 256), *shapes)],
        in_specs=[pl.BlockSpec(memory_space=pltpu.SMEM)] + [anywhere] * count,
        out_specs=[anywhere] * (count + 1),
        scratch_shapes=[
            pltpu.VMEM((rows, 256), BF16),
            *(pltpu.VMEM(shape[1:], BF16) for shape in shapes),
            pltpu.SemaphoreType.DMA((crossing + count,)),
        ],
        name="pack",
    )(core.reshape(1), *weights)
    return stacks, sent


def unpacked(stacks, received):
    count = len(stacks)
    crossing = sum(s.shape[1] * (s.shape[3] // 256) for s in stacks)
    anywhere = pl.BlockSpec(memory_space=pl.ANY)
    return pl.pallas_call(
        functools.partial(_unpack_kernel, count=count),
        out_shape=[jax.ShapeDtypeStruct(s.shape, BF16) for s in stacks],
        in_specs=[pl.BlockSpec(memory_space=pltpu.VMEM)] + [anywhere] * count,
        out_specs=[anywhere] * count,
        input_output_aliases={i + 1: i for i in range(count)},
        scratch_shapes=[pltpu.SemaphoreType.DMA((crossing,))],
        name="unpack",
    )(pltpu.with_memory_space_constraint(received, pltpu.VMEM), *stacks)


def to_pieces(value, count, width):
    lead = value.size // value.shape[-1] // 8
    blocks = value.reshape(lead, 8, -1, width).transpose(0, 2, 1, 3).reshape(-1, 8, width)
    spare = count - blocks.shape[0]
    if spare:
        blocks = jnp.concatenate([blocks, jnp.zeros((spare, 8, width), blocks.dtype)], axis=0)
    return blocks


def from_pieces(blocks, shape):
    width = blocks.shape[-1]
    across = shape[-1] // width
    lead = 1
    for size in shape[:-1]:
        lead *= size
    used = blocks[: lead // 8 * across]
    return used.reshape(lead // 8, across, 8, width).transpose(0, 2, 1, 3).reshape(shape)


def mass_partial(window, column, mass_vals):
    modes = window.shape[0]
    picked = window.reshape(modes, -1, BLOCK)[:, column, :]
    product = jnp.einsum("mrei,reoi->mro", picked, mass_vals, preferred_element_type=F32)
    return product.reshape(modes, -1)


def _unpaired_kernel(grams, stiff, mass, *, n_mass, n_stiff):
    modes = mass.shape[1]
    every = jnp.sum(grams[:, :n_mass, :].astype(F32), axis=0)
    mass[:n_mass] = every[:, :modes]
    mass[n_mass:] = every[:, modes:]
    for layer in range(grams.shape[0] // 2):
        rows = slice(n_mass, n_mass + 8)
        pair = grams[2 * layer, rows, :].astype(F32) + grams[2 * layer + 1, rows, :].astype(F32)
        at = 2 * n_stiff * layer
        stiff[at : at + n_stiff] = pair[:n_stiff, :modes]
        stiff[at + n_stiff : at + 2 * n_stiff] = pair[:n_stiff, modes:]


def unpaired(grams, n_mass, n_stiff):
    modes = grams.shape[2] // 2
    return pl.pallas_call(
        functools.partial(_unpaired_kernel, n_mass=n_mass, n_stiff=n_stiff),
        out_shape=[jax.ShapeDtypeStruct((modes, modes), F32)] * 2,
        in_specs=[pl.BlockSpec(memory_space=pltpu.VMEM)],
        name="unpaired",
    )(pltpu.with_memory_space_constraint(grams, pltpu.VMEM))


def per_device(
    modes_root,
    modes_mid,
    modes_low,
    factor_root,
    factor_mid,
    factor_low,
    update_mid,
    update_low,
    map_mid,
    map_low,
    mass_vals,
    mass_cols,
):
    owner = lax.axis_index("subtree")
    core = lax.axis_index("core")
    owners = lax.axis_size("subtree")
    layers = lax.axis_size("z")
    modes = modes_root.shape[1]
    w_root, w_mid, w_low = modes_root.shape[2], modes_mid.shape[2], modes_low.shape[2]
    b_root, b_mid, b_low = w_root // BLOCK, w_mid // BLOCK, w_low // BLOCK
    local_blocks = b_root + 2 * b_mid + 4 * b_low
    b_own = b_mid + 2 * b_low
    w_own = b_own * BLOCK

    def half(value, which, axis=0):
        size = value.shape[axis] // 2
        return lax.dynamic_slice_in_dim(value, which * size, size, axis)

    column = mass_cols - (owner - 1) * local_blocks
    place = column // local_blocks
    block = column % local_blocks
    is_low = block >= b_root + 2 * b_mid
    after_root = block - b_root
    low_block = after_root - 2 * b_mid
    of = jnp.where(is_low, low_block // (2 * b_low), after_root // b_mid)
    within = jnp.where(is_low, b_mid + low_block % (2 * b_low), after_root % b_mid)
    b_window = b_root + b_own
    mine = jnp.where(block < b_root, block, b_root + within) + place * b_window
    theirs = 3 * b_window + place * b_own + within
    column_after = jnp.where((block < b_root) | (of == core), mine, theirs)
    t_mid = half(map_mid, core)[:, 0] - owner * local_blocks
    t_low = half(map_low, core)[:, 0] - owner * local_blocks
    first_mid = b_root + core * b_mid

    def forward(stack, right, *held):
        part = jnp.einsum("hnij,mnj->hnmi", stack, right, preferred_element_type=F32)
        width = part.size // owners // 8
        return scatter_sum(to_pieces(part.astype(BF16), owners, width), "subtree", *held)

    def whole(piece, shape, *held):
        got, *held = gather(piece.astype(BF16), "subtree", *held)
        return from_pieces(got, shape), *held

    def update_term(stack, y, *held):
        part = jnp.einsum("hnai,hnmi->nma", stack, y, preferred_element_type=F32)
        return full_sum(part, "z", *held)

    def placed(term, target, count):
        blocks = []
        for index in range(count):
            hit = (target == index)[:, None, None]
            blocks.append(jnp.sum(jnp.where(hit, term, 0.0), axis=0))
        return jnp.concatenate(blocks, axis=1)

    def back_term(stack, candidates, *held):
        g = jnp.zeros((stack.shape[1], modes, BLOCK), BF16)
        for hit, block in candidates:
            g = jnp.where(hit[:, None, None], block[None], g)
        part = jnp.einsum("hnai,nma->hnmi", stack, g, preferred_element_type=F32)
        width = part.size // owners // 8
        return scatter_sum(to_pieces(part.astype(BF16), owners, width), "subtree", *held)

    def transposed(stack, d, *held):
        part = jnp.einsum("hnij,hnmi->nmj", stack, d, preferred_element_type=F32)
        return full_sum(jnp.transpose(part, (1, 0, 2)).reshape(modes, -1), "z", *held)

    def cut(flat, target, count):
        return [(target == i, flat[:, i * BLOCK : (i + 1) * BLOCK]) for i in range(count)]

    stacked = side_by_side(modes_root, modes_mid, modes_low)
    layer = lax.axis_index("z")
    t_own = t_low - first_mid
    before, after, t_mid, t_low, t_own, column_after, layer = lax.optimization_barrier(
        (*neighbours(stacked), t_mid, t_low, t_own, column_after, layer)
    )
    window = jnp.concatenate([before, stacked, after], axis=1)
    z_part = mass_partial(window, column, mass_vals).astype(BF16)

    def of_core(flat, which):
        mid = w_root + which * w_mid
        low = w_root + 2 * w_mid + which * 2 * w_low
        return jnp.concatenate(
            [flat[:, :w_root], flat[:, mid : mid + w_mid], flat[:, low : low + 2 * w_low]], axis=1
        )

    parts = of_core(z_part, 0), of_core(z_part, 1)
    own = jnp.where(core == 0, parts[0], parts[1])
    z_part = own.astype(F32) + swap(jnp.where(core == 0, parts[1], parts[0])).astype(F32)
    tiles = jnp.transpose(
        z_part.astype(BF16).reshape(layers, modes // layers, b_root + b_own, BLOCK), (0, 2, 1, 3)
    )
    b_rest = b_root + b_mid
    rest = tiles[:, :b_rest]
    lower = tiles[:, b_rest:].reshape(1, -1, modes // layers, BLOCK)
    n_lower = lower.shape[1]
    pieces = jnp.concatenate([jnp.broadcast_to(lower, (layers, *lower.shape[1:])), rest], axis=1)

    pieces, core = lax.optimization_barrier((pieces, core))
    stacks, sent = split_nodes(core, factor_low, factor_mid, update_low, update_mid)
    sent, root_sent = lax.optimization_barrier((sent, factor_root[0]))
    received, root_received = lax.optimization_barrier((swap(sent), swap(root_sent)))
    factors_root = (factor_root[0], root_received)
    (z,) = scatter_sum(pieces, "z")
    f_low, f_mid, u_low, u_mid = unpacked(stacks, received)

    def from_tiles(value, lead):
        across = value.shape[-3]
        return jnp.transpose(value, (*range(lead), lead + 1, lead, lead + 2)).reshape(
            -1, across * BLOCK
        )

    z = z.astype(BF16)
    z_low = from_tiles(z[:n_lower].reshape(layers, -1, *z.shape[1:]), 1)
    z_low, z_rest = lax.optimization_barrier((z_low, z[n_lower:]))

    y_low, t_low, t_own = forward(f_low, z_low.reshape(modes, 2, w_low), t_low, t_own)
    y, t_low, t_own = whole(y_low, (2, 2, modes, f_low.shape[-2]), t_low, t_own)
    part = jnp.einsum("hnai,hnmi->nma", u_low, y, preferred_element_type=F32).astype(BF16)
    tiles = jnp.concatenate([part.reshape(-1, *z_rest.shape[1:]), z_rest], axis=0)
    got, t_low, t_own = gather(tiles, "z", t_low, t_own)
    term = total(got[:, : -b_rest]).reshape(part.shape)
    z_rest = from_tiles(got[:, -b_rest:], 1)
    z_root, z_mid = z_rest[:, :w_root], z_rest[:, w_root:]
    acc_mid = placed(term, t_own, b_mid)
    acc_root = placed(term, t_low, b_root)
    right = (z_mid.astype(F32) - acc_mid).astype(BF16)
    right, acc_root, z_root, z_mid = lax.optimization_barrier((right, acc_root, z_root, z_mid))
    y_mid, t_mid = forward(f_mid, right.reshape(modes, 1, w_mid), t_mid)
    y, t_mid = whole(y_mid, (2, 1, modes, f_mid.shape[-2]), t_mid)
    term, t_mid, acc_root = update_term(u_mid, y, t_mid, acc_root)
    acc_root = acc_root + placed(term, t_mid, b_root)

    half_modes = modes // 2
    z_root, t_mid, core = lax.optimization_barrier((z_root, t_mid, core))

    def of_modes(value, which):
        return lax.dynamic_slice_in_dim(value, which * half_modes, half_modes, 0)

    acc_root = of_modes(acc_root, core) + swap(of_modes(acc_root, 1 - core))
    right = (of_modes(z_root, core).astype(F32) - acc_root).astype(BF16)

    def by_core(mine, other):
        return jnp.concatenate(
            [jnp.where(core == 0, mine, other), jnp.where(core == 0, other, mine)], axis=0
        )

    part = jnp.stack(
        [jnp.einsum("ij,mj->mi", f, right, preferred_element_type=F32) for f in factors_root]
    )
    (y_root,) = scatter_sum(to_pieces(part.astype(BF16), owners, 2 * BLOCK), "subtree")

    d_root, t_mid, core = whole(y_root, part.shape, t_mid, core)
    part = sum(
        jnp.einsum("ij,mi->mj", f, d, preferred_element_type=F32)
        for f, d in zip(factors_root, d_root)
    )
    s_half, t_mid, core = full_sum(part, "z", t_mid, core)
    s_other = swap(s_half)
    x_root = by_core(s_half.astype(BF16), s_other.astype(BF16))
    x_root = lax.optimization_barrier(x_root)
    root_blocks = cut(x_root, t_mid, b_root)
    v_mid, y_mid, x_root = back_term(u_mid, root_blocks, y_mid, x_root)
    d_mid, x_root = whole(y_mid - v_mid, (2, 1, modes, f_mid.shape[-2]), x_root)
    s_mid, x_root, t_low, t_own = transposed(f_mid, d_mid, x_root, t_low, t_own)
    x_mid = s_mid.astype(BF16)
    blocks = cut(x_root, t_low, b_root) + cut(x_mid, t_own, b_mid)
    v_low, y_low, x_mid, x_root = back_term(u_low, blocks, y_low, x_mid, x_root)
    d_low, x_mid, x_root = whole(y_low - v_low, (2, 2, modes, f_low.shape[-2]), x_mid, x_root)
    s_low, x_mid, x_root, s_half, s_other, column_after, core, layer = transposed(
        f_low, d_low, x_mid, x_root, s_half, s_other, column_after, core, layer
    )
    x_low = s_low.astype(BF16)

    y_own = jnp.concatenate([x_root, x_mid, x_low], axis=1)
    before, after = neighbours(y_own)
    others = swap(jnp.concatenate([part[:, w_root:] for part in (before, y_own, after)], axis=1))
    window = jnp.concatenate([before, y_own, after, others], axis=1)
    my_part = mass_partial(window, column_after, mass_vals).astype(BF16)

    other = others[:, w_own : 2 * w_own]
    own = y_own[:, w_root:]
    first = jnp.where(core == 0, own, other)
    second = jnp.where(core == 0, other, own)
    y_all = jnp.concatenate(
        [x_root, first[:, :w_mid], second[:, :w_mid], first[:, w_mid:], second[:, w_mid:]], axis=1
    )

    mass_part = jnp.einsum("jr,kr->jk", y_all, my_part, preferred_element_type=F32)
    size = modes // layers
    y_mine = lax.dynamic_slice_in_dim(y_own, layer * size, size, axis=0)
    rows = lax.broadcasted_iota(jnp.int32, y_mine.shape, 1)
    y_mine = jnp.where((core == 0) | (rows >= w_root), y_mine, 0).astype(BF16)
    z = jnp.concatenate([z_root, z_mid, z_low], axis=1)
    stiff_part = jnp.einsum("jr,kr->jk", y_mine, z, preferred_element_type=F32)

    def paired(value):
        size = value.shape[0] // 2
        return jnp.concatenate([value[:size], value[size:]], axis=1)

    n_mass, n_stiff = modes // 2, size // 2
    grams = jnp.concatenate([paired(mass_part), paired(stiff_part)], axis=0)
    grams = jnp.pad(grams, ((0, -(n_mass + n_stiff) % 8), (0, 0)))
    grams, y_all, s_half, s_other = full_sum(grams, "subtree", y_all, s_half, s_other)
    (grams,) = gather(grams.astype(BF16), FRONT)
    stiff, mass = unpaired(grams, n_mass, n_stiff)

    def output(flat, count):
        return jnp.transpose(flat.reshape(modes, count, -1), (1, 0, 2)).astype(F32)

    low_from = w_root + 2 * w_mid
    solved_root = by_core(s_half, s_other)[None]
    solved_mid = output(y_all[:, w_root:low_from], 2)
    solved_low = output(y_all[:, low_from:], 4)
    return solved_root, solved_mid, solved_low, stiff, mass


def solution(mesh):
    owners, fronts = mesh.shape["subtree"], mesh.shape["front"]
    split = Mesh(mesh.devices.reshape(owners, fronts // 2, 2), ("subtree", *FRONT))
    factor = P(None, FRONT, "subtree")
    update = P(None, "subtree", FRONT)
    rows = P(None, None, "subtree")

    return jax.shard_map(
        per_device,
        mesh=split,
        in_specs=(
            rows,
            rows,
            rows,
            factor,
            factor,
            factor,
            update,
            update,
            P(None, "subtree"),
            P(None, "subtree"),
            P("subtree", FRONT, None, None),
            P("subtree", FRONT),
        ),
        out_specs=(rows, rows, rows, P(), P()),
        check_vma=False,
    )
```

```python
import functools

import jax
import jax.numpy as jnp
from jax import lax
from jax.experimental import pallas as pl
from jax.experimental.pallas import tpu as pltpu
from jax.sharding import Mesh, PartitionSpec as P


BLOCK = 128
F32 = jnp.float32
BF16 = jnp.bfloat16
FRONT = ("z", "core")


def total(parts):
    return jnp.sum(parts.astype(F32), axis=0)


def exchange(pieces, axis, held):
    return lax.optimization_barrier((lax.all_to_all(pieces, axis, 0, 0), *held))


def gather(piece, axis, *held):
    copies = jnp.broadcast_to(piece[None], (lax.axis_size(axis), *piece.shape))
    return exchange(copies, axis, held)


def scatter_sum(pieces, axis, *held):
    got, *held = exchange(pieces.astype(BF16), axis, held)
    return total(got), *held


def full_sum(part, axis, *held):
    got, *held = gather(part.astype(BF16), axis, *held)
    return total(got), *held


def swap(value):
    return lax.ppermute(value, "core", [(0, 1), (1, 0)])


def neighbours(flat):
    count = lax.axis_size("subtree")
    before = lax.ppermute(flat, "subtree", [(i, i + 1) for i in range(count - 1)])
    after = lax.ppermute(flat, "subtree", [(i + 1, i) for i in range(count - 1)])
    return before, after


def _lanes(width):
    return [slice(at, at + 256) for at in range(0, width, 256)]


def _run(moves, sems):
    copies = [pltpu.make_async_copy(*move, sems.at[i]) for i, move in enumerate(moves)]
    for copy in copies:
        copy.start()
    for copy in copies:
        copy.wait()


def _pack_kernel(core_ref, *refs, count):
    weights, sent, stacks = refs[:count], refs[count], refs[count + 1 : 2 * count + 1]
    staged, halves, sems = refs[2 * count + 1], refs[2 * count + 2 : -1], refs[-1]
    core = core_ref[0]
    moves = []
    row = 0
    for weight, half in zip(weights, halves):
        nodes, rows, width = half.shape
        moves.append((weight.at[pl.ds(core * nodes, nodes)], half))
        for node in range(nodes):
            for lanes in _lanes(width):
                source = weight.at[(1 - core) * nodes + node, :, lanes]
                moves.append((source, staged.at[row : row + rows]))
                row += rows
    _run(moves, sems)
    out = [(half, stack.at[0]) for half, stack in zip(halves, stacks)]
    _run([(staged, sent), *out], sems)


def _unpack_kernel(received, *refs, count):
    stacks, sems = refs[count : 2 * count], refs[-1]
    moves = []
    row = 0
    for stack in stacks:
        nodes, rows, width = stack.shape[1:]
        for node in range(nodes):
            for lanes in _lanes(width):
                moves.append((received.at[row : row + rows], stack.at[1, node, :, lanes]))
                row += rows
    _run(moves, sems)


def _side_by_side_kernel(*refs):
    levels, flat, sems = refs[:-2], refs[-2], refs[-1]
    moves = []
    at = 0
    for level in levels:
        nodes, _, width = level.shape
        for node in range(nodes):
            moves.append((level.at[node], flat.at[:, at : at + width]))
            at += width
    _run(moves, sems)


def side_by_side(*levels):
    width = sum(level.shape[0] * level.shape[2] for level in levels)
    return pl.pallas_call(
        _side_by_side_kernel,
        out_shape=jax.ShapeDtypeStruct((levels[0].shape[1], width), BF16),
        in_specs=[pl.BlockSpec(memory_space=pl.ANY)] * len(levels),
        out_specs=pl.BlockSpec(memory_space=pltpu.VMEM),
        scratch_shapes=[pltpu.SemaphoreType.DMA((sum(level.shape[0] for level in levels),))],
        name="side_by_side",
    )(*levels)


def split_nodes(core, *weights):
    count = len(weights)
    shapes = [(2, w.shape[0] // 2, *w.shape[1:]) for w in weights]
    crossing = sum(n * (width // 256) for _, n, _, width in shapes)
    rows = sum(n * r * (width // 256) for _, n, r, width in shapes)
    anywhere = pl.BlockSpec(memory_space=pl.ANY)
    sent, *stacks = pl.pallas_call(
        functools.partial(_pack_kernel, count=count),
        out_shape=[jax.ShapeDtypeStruct(shape, BF16) for shape in ((rows, 256), *shapes)],
        in_specs=[pl.BlockSpec(memory_space=pltpu.SMEM)] + [anywhere] * count,
        out_specs=[anywhere] * (count + 1),
        scratch_shapes=[
            pltpu.VMEM((rows, 256), BF16),
            *(pltpu.VMEM(shape[1:], BF16) for shape in shapes),
            pltpu.SemaphoreType.DMA((crossing + count,)),
        ],
        name="pack",
    )(core.reshape(1), *weights)
    return stacks, swap(sent)


def unpacked(stacks, received):
    count = len(stacks)
    crossing = sum(s.shape[1] * (s.shape[3] // 256) for s in stacks)
    anywhere = pl.BlockSpec(memory_space=pl.ANY)
    return pl.pallas_call(
        functools.partial(_unpack_kernel, count=count),
        out_shape=[jax.ShapeDtypeStruct(s.shape, BF16) for s in stacks],
        in_specs=[pl.BlockSpec(memory_space=pltpu.VMEM)] + [anywhere] * count,
        out_specs=[anywhere] * count,
        input_output_aliases={i + 1: i for i in range(count)},
        scratch_shapes=[pltpu.SemaphoreType.DMA((crossing,))],
        name="unpack",
    )(pltpu.with_memory_space_constraint(received, pltpu.VMEM), *stacks)


def to_pieces(value, count, width):
    lead = value.size // value.shape[-1] // 8
    blocks = value.reshape(lead, 8, -1, width).transpose(0, 2, 1, 3).reshape(-1, 8, width)
    spare = count - blocks.shape[0]
    if spare:
        blocks = jnp.concatenate([blocks, jnp.zeros((spare, 8, width), blocks.dtype)], axis=0)
    return blocks


def from_pieces(blocks, shape):
    width = blocks.shape[-1]
    across = shape[-1] // width
    lead = 1
    for size in shape[:-1]:
        lead *= size
    used = blocks[: lead // 8 * across]
    return used.reshape(lead // 8, across, 8, width).transpose(0, 2, 1, 3).reshape(shape)


def mass_partial(window, column, mass_vals):
    modes = window.shape[0]
    picked = window.reshape(modes, -1, BLOCK)[:, column, :]
    product = jnp.einsum("mrei,reoi->mro", picked, mass_vals, preferred_element_type=F32)
    return product.reshape(modes, -1)


def _unpaired_kernel(grams, stiff, mass, *, n_mass, n_stiff):
    modes = mass.shape[1]
    every = jnp.sum(grams[:, :n_mass, :].astype(F32), axis=0)
    mass[:n_mass] = every[:, :modes]
    mass[n_mass:] = every[:, modes:]
    for layer in range(grams.shape[0] // 2):
        rows = slice(n_mass, n_mass + 8)
        pair = grams[2 * layer, rows, :].astype(F32) + grams[2 * layer + 1, rows, :].astype(F32)
        at = 2 * n_stiff * layer
        stiff[at : at + n_stiff] = pair[:n_stiff, :modes]
        stiff[at + n_stiff : at + 2 * n_stiff] = pair[:n_stiff, modes:]


def unpaired(grams, n_mass, n_stiff):
    modes = grams.shape[2] // 2
    return pl.pallas_call(
        functools.partial(_unpaired_kernel, n_mass=n_mass, n_stiff=n_stiff),
        out_shape=[jax.ShapeDtypeStruct((modes, modes), F32)] * 2,
        in_specs=[pl.BlockSpec(memory_space=pltpu.VMEM)],
        name="unpaired",
    )(pltpu.with_memory_space_constraint(grams, pltpu.VMEM))


def per_device(
    modes_root,
    modes_mid,
    modes_low,
    factor_root,
    factor_mid,
    factor_low,
    update_mid,
    update_low,
    map_mid,
    map_low,
    mass_vals,
    mass_cols,
):
    owner = lax.axis_index("subtree")
    core = lax.axis_index("core")
    owners = lax.axis_size("subtree")
    layers = lax.axis_size("z")
    modes = modes_root.shape[1]
    w_root, w_mid, w_low = modes_root.shape[2], modes_mid.shape[2], modes_low.shape[2]
    b_root, b_mid, b_low = w_root // BLOCK, w_mid // BLOCK, w_low // BLOCK
    local_blocks = b_root + 2 * b_mid + 4 * b_low
    b_own = b_mid + 2 * b_low
    w_own = b_own * BLOCK
    mid_at, low_at = w_root, w_root + w_mid

    def half(value, which, axis=0):
        size = value.shape[axis] // 2
        return lax.dynamic_slice_in_dim(value, which * size, size, axis)

    stacked, root_sent, map_mid, map_low, mass_cols = lax.optimization_barrier(
        (
            side_by_side(modes_root, modes_mid, modes_low),
            factor_root[0],
            map_mid,
            map_low,
            mass_cols,
        )
    )

    column = mass_cols - (owner - 1) * local_blocks
    place = column // local_blocks
    block = column % local_blocks
    is_low = block >= b_root + 2 * b_mid
    after_root = block - b_root
    low_block = after_root - 2 * b_mid
    of = jnp.where(is_low, low_block // (2 * b_low), after_root // b_mid)
    within = jnp.where(is_low, b_mid + low_block % (2 * b_low), after_root % b_mid)
    b_window = b_root + b_own
    mine = jnp.where(block < b_root, block, b_root + within) + place * b_window
    theirs = 3 * b_window + place * b_own + within
    column_after = jnp.where((block < b_root) | (of == core), mine, theirs)
    t_mid = half(map_mid, core)[:, 0] - owner * local_blocks
    t_low = half(map_low, core)[:, 0] - owner * local_blocks
    first_mid = b_root + core * b_mid

    def forward(stack, right, *held):
        part = jnp.einsum("hnij,mnj->hnmi", stack, right, preferred_element_type=F32)
        width = part.size // owners // 8
        return scatter_sum(to_pieces(part.astype(BF16), owners, width), "subtree", *held)

    def whole(piece, shape, *held):
        got, *held = gather(piece.astype(BF16), "subtree", *held)
        return from_pieces(got, shape), *held

    def update_term(stack, y, *held):
        part = jnp.einsum("hnai,hnmi->nma", stack, y, preferred_element_type=F32)
        return full_sum(part, "z", *held)

    def placed(term, target, count):
        blocks = []
        for index in range(count):
            hit = (target == index)[:, None, None]
            blocks.append(jnp.sum(jnp.where(hit, term, 0.0), axis=0))
        return jnp.concatenate(blocks, axis=1)

    def back_term(stack, candidates, *held):
        g = jnp.zeros((stack.shape[1], modes, BLOCK), BF16)
        for hit, block in candidates:
            g = jnp.where(hit[:, None, None], block[None], g)
        part = jnp.einsum("hnai,nma->hnmi", stack, g, preferred_element_type=F32)
        width = part.size // owners // 8
        return scatter_sum(to_pieces(part.astype(BF16), owners, width), "subtree", *held)

    def transposed(stack, d, *held):
        part = jnp.einsum("hnij,hnmi->nmj", stack, d, preferred_element_type=F32)
        return full_sum(jnp.transpose(part, (1, 0, 2)).reshape(modes, -1), "z", *held)

    def cut(flat, target, count):
        return [(target == i, flat[:, i * BLOCK : (i + 1) * BLOCK]) for i in range(count)]

    layer = lax.axis_index("z")
    t_own = t_low - first_mid
    before, after = neighbours(stacked)
    root_received = swap(root_sent)
    before, after, root_received, t_mid, t_low, t_own, column_after, layer = (
        lax.optimization_barrier(
            (before, after, root_received, t_mid, t_low, t_own, column_after, layer)
        )
    )
    factors_root = (factor_root[0], root_received)
    window = jnp.concatenate([before, stacked, after], axis=1)
    z_part = mass_partial(window, column, mass_vals).astype(BF16)

    def of_core(flat, which):
        mid = w_root + which * w_mid
        low = w_root + 2 * w_mid + which * 2 * w_low
        return jnp.concatenate(
            [flat[:, :w_root], flat[:, mid : mid + w_mid], flat[:, low : low + 2 * w_low]], axis=1
        )

    z_part = jnp.stack([of_core(z_part, 0), of_core(z_part, 1)]).reshape(
        2, layers, modes // layers, w_root + w_own
    )
    z_part = jnp.transpose(z_part, (1, 0, 2, 3)).reshape(2 * layers, *z_part.shape[2:])
    z_part, core = lax.optimization_barrier((z_part, core))
    stacks, received = split_nodes(core, factor_low, factor_mid, update_low, update_mid)
    (z_mine,) = scatter_sum(z_part, FRONT)
    f_low, f_mid, u_low, u_mid = unpacked(stacks, received)
    (z,) = gather(z_mine.astype(BF16), "z")
    z = z.reshape(modes, -1)

    right = z[:, low_at:].reshape(modes, 2, w_low)
    y_low, t_low, t_own = forward(f_low, right, t_low, t_own)
    y, t_low, t_own = whole(y_low, (2, 2, modes, f_low.shape[-2]), t_low, t_own)
    term, t_low, t_own = update_term(u_low, y, t_low, t_own)
    acc_mid = placed(term, t_own, b_mid)
    acc_root = placed(term, t_low, b_root)
    right = (z[:, mid_at:low_at].astype(F32) - acc_mid).astype(BF16)
    right, acc_root = lax.optimization_barrier((right, acc_root))
    y_mid, t_mid = forward(f_mid, right.reshape(modes, 1, w_mid), t_mid)
    y, t_mid = whole(y_mid, (2, 1, modes, f_mid.shape[-2]), t_mid)
    term, t_mid, acc_root = update_term(u_mid, y, t_mid, acc_root)
    acc_root = acc_root + placed(term, t_mid, b_root)

    half_modes = modes // 2
    acc_root, t_mid, core = lax.optimization_barrier((acc_root, t_mid, core))

    def of_modes(value, which):
        return lax.dynamic_slice_in_dim(value, which * half_modes, half_modes, 0)

    acc_root = of_modes(acc_root, core) + swap(of_modes(acc_root, 1 - core))
    z_root = lax.dynamic_slice(z, (core * half_modes, 0), (half_modes, mid_at))
    right = (z_root.astype(F32) - acc_root).astype(BF16)

    def by_core(mine, other):
        return jnp.concatenate(
            [jnp.where(core == 0, mine, other), jnp.where(core == 0, other, mine)], axis=0
        )

    part = jnp.stack(
        [jnp.einsum("ij,mj->mi", f, right, preferred_element_type=F32) for f in factors_root]
    )
    (y_root,) = scatter_sum(to_pieces(part.astype(BF16), owners, 2 * BLOCK), "subtree")

    d_root, t_mid, core = whole(y_root, part.shape, t_mid, core)
    part = sum(
        jnp.einsum("ij,mi->mj", f, d, preferred_element_type=F32)
        for f, d in zip(factors_root, d_root)
    )
    s_half, t_mid, core = full_sum(part, "z", t_mid, core)
    s_other = swap(s_half)
    x_root = by_core(s_half.astype(BF16), s_other.astype(BF16))
    x_root = lax.optimization_barrier(x_root)
    root_blocks = cut(x_root, t_mid, b_root)
    v_mid, y_mid, x_root = back_term(u_mid, root_blocks, y_mid, x_root)
    d_mid, x_root = whole(y_mid - v_mid, (2, 1, modes, f_mid.shape[-2]), x_root)
    s_mid, x_root, t_low, t_own = transposed(f_mid, d_mid, x_root, t_low, t_own)
    x_mid = s_mid.astype(BF16)
    blocks = cut(x_root, t_low, b_root) + cut(x_mid, t_own, b_mid)
    v_low, y_low, x_mid, x_root = back_term(u_low, blocks, y_low, x_mid, x_root)
    d_low, x_mid, x_root = whole(y_low - v_low, (2, 2, modes, f_low.shape[-2]), x_mid, x_root)
    s_low, x_mid, x_root, s_half, s_other, column_after, core, layer = transposed(
        f_low, d_low, x_mid, x_root, s_half, s_other, column_after, core, layer
    )
    x_low = s_low.astype(BF16)

    y_own = jnp.concatenate([x_root, x_mid, x_low], axis=1)
    before, after = neighbours(y_own)
    others = swap(jnp.concatenate([part[:, w_root:] for part in (before, y_own, after)], axis=1))
    window = jnp.concatenate([before, y_own, after, others], axis=1)
    my_part = mass_partial(window, column_after, mass_vals).astype(BF16)

    other = others[:, w_own : 2 * w_own]
    own = y_own[:, w_root:]
    first = jnp.where(core == 0, own, other)
    second = jnp.where(core == 0, other, own)
    y_all = jnp.concatenate(
        [x_root, first[:, :w_mid], second[:, :w_mid], first[:, w_mid:], second[:, w_mid:]], axis=1
    )

    mass_part = jnp.einsum("jr,kr->jk", y_all, my_part, preferred_element_type=F32)
    size = modes // layers
    y_mine = lax.dynamic_slice_in_dim(y_own, layer * size, size, axis=0)
    rows = lax.broadcasted_iota(jnp.int32, y_mine.shape, 1)
    y_mine = jnp.where((core == 0) | (rows >= w_root), y_mine, 0).astype(BF16)
    stiff_part = jnp.einsum("jr,kr->jk", y_mine, z, preferred_element_type=F32)

    def paired(value):
        size = value.shape[0] // 2
        return jnp.concatenate([value[:size], value[size:]], axis=1)

    n_mass, n_stiff = modes // 2, size // 2
    grams = jnp.concatenate([paired(mass_part), paired(stiff_part)], axis=0)
    grams = jnp.pad(grams, ((0, -(n_mass + n_stiff) % 8), (0, 0)))
    grams, y_all, s_half, s_other = full_sum(grams, "subtree", y_all, s_half, s_other)
    (grams,) = gather(grams.astype(BF16), FRONT)
    stiff, mass = unpaired(grams, n_mass, n_stiff)

    def output(flat, count):
        return jnp.transpose(flat.reshape(modes, count, -1), (1, 0, 2)).astype(F32)

    low_from = w_root + 2 * w_mid
    solved_root = by_core(s_half, s_other)[None]
    solved_mid = output(y_all[:, w_root:low_from], 2)
    solved_low = output(y_all[:, low_from:], 4)
    return solved_root, solved_mid, solved_low, stiff, mass


def solution(mesh):
    owners, fronts = mesh.shape["subtree"], mesh.shape["front"]
    split = Mesh(mesh.devices.reshape(owners, fronts // 2, 2), ("subtree", *FRONT))
    factor = P(None, FRONT, "subtree")
    update = P(None, "subtree", FRONT)
    rows = P(None, None, "subtree")

    return jax.shard_map(
        per_device,
        mesh=split,
        in_specs=(
            rows,
            rows,
            rows,
            factor,
            factor,
            factor,
            update,
            update,
            P(None, "subtree"),
            P(None, "subtree"),
            P("subtree", FRONT, None, None),
            P("subtree", FRONT),
        ),
        out_specs=(rows, rows, rows, P(), P()),
        check_vma=False,
    )
```

```python
import functools

import jax
import jax.numpy as jnp
from jax import lax
from jax.experimental import pallas as pl
from jax.experimental.pallas import tpu as pltpu
from jax.sharding import Mesh, PartitionSpec as P


BLOCK = 128
F32 = jnp.float32
BF16 = jnp.bfloat16
FRONT = ("z", "core")


def total(parts):
    return jnp.sum(parts.astype(F32), axis=0)


def exchange(pieces, axis, held):
    return lax.optimization_barrier((lax.all_to_all(pieces, axis, 0, 0), *held))


def gather(piece, axis, *held):
    copies = jnp.broadcast_to(piece[None], (lax.axis_size(axis), *piece.shape))
    return exchange(copies, axis, held)


def scatter_sum(pieces, axis, *held):
    got, *held = exchange(pieces.astype(BF16), axis, held)
    return total(got), *held


def full_sum(part, axis, *held):
    got, *held = gather(part.astype(BF16), axis, *held)
    return total(got), *held


def swap(value):
    return lax.ppermute(value, "core", [(0, 1), (1, 0)])


def neighbours(flat):
    count = lax.axis_size("subtree")
    before = lax.ppermute(flat, "subtree", [(i, i + 1) for i in range(count - 1)])
    after = lax.ppermute(flat, "subtree", [(i + 1, i) for i in range(count - 1)])
    return before, after


def _lanes(width):
    return [slice(at, at + 256) for at in range(0, width, 256)]


def _run(moves, sems):
    copies = [pltpu.make_async_copy(*move, sems.at[i]) for i, move in enumerate(moves)]
    for copy in copies:
        copy.start()
    for copy in copies:
        copy.wait()


def _pack_kernel(core_ref, *refs, count):
    weights, sent, stacks = refs[:count], refs[count], refs[count + 1 : 2 * count + 1]
    staged, halves, sems = refs[2 * count + 1], refs[2 * count + 2 : -1], refs[-1]
    core = core_ref[0]
    moves = []
    row = 0
    for weight, half in zip(weights, halves):
        nodes, rows, width = half.shape
        moves.append((weight.at[pl.ds(core * nodes, nodes)], half))
        for node in range(nodes):
            for lanes in _lanes(width):
                source = weight.at[(1 - core) * nodes + node, :, lanes]
                moves.append((source, staged.at[row : row + rows]))
                row += rows
    _run(moves, sems)
    out = [(half, stack.at[0]) for half, stack in zip(halves, stacks)]
    _run([(staged, sent), *out], sems)


def _unpack_kernel(received, *refs, count):
    stacks, sems = refs[count : 2 * count], refs[-1]
    moves = []
    row = 0
    for stack in stacks:
        nodes, rows, width = stack.shape[1:]
        for node in range(nodes):
            for lanes in _lanes(width):
                moves.append((received.at[row : row + rows], stack.at[1, node, :, lanes]))
                row += rows
    _run(moves, sems)


def _side_by_side_kernel(*refs):
    levels, flat, sems = refs[:-2], refs[-2], refs[-1]
    moves = []
    at = 0
    for level in levels:
        nodes, _, width = level.shape
        for node in range(nodes):
            moves.append((level.at[node], flat.at[:, at : at + width]))
            at += width
    _run(moves, sems)


def side_by_side(*levels):
    width = sum(level.shape[0] * level.shape[2] for level in levels)
    return pl.pallas_call(
        _side_by_side_kernel,
        out_shape=jax.ShapeDtypeStruct((levels[0].shape[1], width), BF16),
        in_specs=[pl.BlockSpec(memory_space=pl.ANY)] * len(levels),
        out_specs=pl.BlockSpec(memory_space=pltpu.VMEM),
        scratch_shapes=[pltpu.SemaphoreType.DMA((sum(level.shape[0] for level in levels),))],
        name="side_by_side",
    )(*levels)


def split_nodes(core, *weights):
    count = len(weights)
    shapes = [(2, w.shape[0] // 2, *w.shape[1:]) for w in weights]
    crossing = sum(n * (width // 256) for _, n, _, width in shapes)
    rows = sum(n * r * (width // 256) for _, n, r, width in shapes)
    anywhere = pl.BlockSpec(memory_space=pl.ANY)
    sent, *stacks = pl.pallas_call(
        functools.partial(_pack_kernel, count=count),
        out_shape=[jax.ShapeDtypeStruct(shape, BF16) for shape in ((rows, 256), *shapes)],
        in_specs=[pl.BlockSpec(memory_space=pltpu.SMEM)] + [anywhere] * count,
        out_specs=[anywhere] * (count + 1),
        scratch_shapes=[
            pltpu.VMEM((rows, 256), BF16),
            *(pltpu.VMEM(shape[1:], BF16) for shape in shapes),
            pltpu.SemaphoreType.DMA((crossing + count,)),
        ],
        name="pack",
    )(core.reshape(1), *weights)
    return stacks, swap(sent)


def unpacked(stacks, received):
    count = len(stacks)
    crossing = sum(s.shape[1] * (s.shape[3] // 256) for s in stacks)
    anywhere = pl.BlockSpec(memory_space=pl.ANY)
    return pl.pallas_call(
        functools.partial(_unpack_kernel, count=count),
        out_shape=[jax.ShapeDtypeStruct(s.shape, BF16) for s in stacks],
        in_specs=[pl.BlockSpec(memory_space=pltpu.VMEM)] + [anywhere] * count,
        out_specs=[anywhere] * count,
        input_output_aliases={i + 1: i for i in range(count)},
        scratch_shapes=[pltpu.SemaphoreType.DMA((crossing,))],
        name="unpack",
    )(pltpu.with_memory_space_constraint(received, pltpu.VMEM), *stacks)


def to_pieces(value, count, width):
    lead = value.size // value.shape[-1] // 8
    blocks = value.reshape(lead, 8, -1, width).transpose(0, 2, 1, 3).reshape(-1, 8, width)
    spare = count - blocks.shape[0]
    if spare:
        blocks = jnp.concatenate([blocks, jnp.zeros((spare, 8, width), blocks.dtype)], axis=0)
    return blocks


def from_pieces(blocks, shape):
    width = blocks.shape[-1]
    across = shape[-1] // width
    lead = 1
    for size in shape[:-1]:
        lead *= size
    used = blocks[: lead // 8 * across]
    return used.reshape(lead // 8, across, 8, width).transpose(0, 2, 1, 3).reshape(shape)


def mass_partial(window, column, mass_vals):
    modes = window.shape[0]
    picked = window.reshape(modes, -1, BLOCK)[:, column, :]
    product = jnp.einsum("mrei,reoi->mro", picked, mass_vals, preferred_element_type=F32)
    return product.reshape(modes, -1)


def _unpaired_kernel(grams, stiff, mass, *, n_mass, n_stiff):
    modes = mass.shape[1]
    every = jnp.sum(grams[:, :n_mass, :].astype(F32), axis=0)
    mass[:n_mass] = every[:, :modes]
    mass[n_mass:] = every[:, modes:]
    for layer in range(grams.shape[0] // 2):
        rows = slice(n_mass, n_mass + 8)
        pair = grams[2 * layer, rows, :].astype(F32) + grams[2 * layer + 1, rows, :].astype(F32)
        at = 2 * n_stiff * layer
        stiff[at : at + n_stiff] = pair[:n_stiff, :modes]
        stiff[at + n_stiff : at + 2 * n_stiff] = pair[:n_stiff, modes:]


def unpaired(grams, n_mass, n_stiff):
    modes = grams.shape[2] // 2
    return pl.pallas_call(
        functools.partial(_unpaired_kernel, n_mass=n_mass, n_stiff=n_stiff),
        out_shape=[jax.ShapeDtypeStruct((modes, modes), F32)] * 2,
        in_specs=[pl.BlockSpec(memory_space=pltpu.VMEM)],
        name="unpaired",
    )(pltpu.with_memory_space_constraint(grams, pltpu.VMEM))


def per_device(
    modes_root,
    modes_mid,
    modes_low,
    factor_root,
    factor_mid,
    factor_low,
    update_mid,
    update_low,
    map_mid,
    map_low,
    mass_vals,
    mass_cols,
):
    owner = lax.axis_index("subtree")
    core = lax.axis_index("core")
    owners = lax.axis_size("subtree")
    layers = lax.axis_size("z")
    modes = modes_root.shape[1]
    w_root, w_mid, w_low = modes_root.shape[2], modes_mid.shape[2], modes_low.shape[2]
    b_root, b_mid, b_low = w_root // BLOCK, w_mid // BLOCK, w_low // BLOCK
    local_blocks = b_root + 2 * b_mid + 4 * b_low
    b_own = b_mid + 2 * b_low
    w_own = b_own * BLOCK
    mid_at, low_at = w_root, w_root + w_mid

    def half(value, which, axis=0):
        size = value.shape[axis] // 2
        return lax.dynamic_slice_in_dim(value, which * size, size, axis)

    stacked, root_sent, map_mid, map_low, mass_cols = lax.optimization_barrier(
        (
            side_by_side(modes_root, modes_mid, modes_low),
            factor_root[0],
            map_mid,
            map_low,
            mass_cols,
        )
    )

    column = mass_cols - (owner - 1) * local_blocks
    place = column // local_blocks
    block = column % local_blocks
    is_low = block >= b_root + 2 * b_mid
    after_root = block - b_root
    low_block = after_root - 2 * b_mid
    of = jnp.where(is_low, low_block // (2 * b_low), after_root // b_mid)
    within = jnp.where(is_low, b_mid + low_block % (2 * b_low), after_root % b_mid)
    b_window = b_root + b_own
    mine = jnp.where(block < b_root, block, b_root + within) + place * b_window
    theirs = 3 * b_window + place * b_own + within
    column_after = jnp.where((block < b_root) | (of == core), mine, theirs)
    t_mid = half(map_mid, core)[:, 0] - owner * local_blocks
    t_low = half(map_low, core)[:, 0] - owner * local_blocks
    first_mid = b_root + core * b_mid

    def forward(stack, right, *held):
        part = jnp.einsum("hnij,mnj->hnmi", stack, right, preferred_element_type=F32)
        width = part.size // owners // 8
        return scatter_sum(to_pieces(part.astype(BF16), owners, width), "subtree", *held)

    def whole(piece, shape, *held):
        got, *held = gather(piece.astype(BF16), "subtree", *held)
        return from_pieces(got, shape), *held

    def update_term(stack, y, *held):
        part = jnp.einsum("hnai,hnmi->nma", stack, y, preferred_element_type=F32)
        return full_sum(part, "z", *held)

    def placed(term, target, count):
        blocks = []
        for index in range(count):
            hit = (target == index)[:, None, None]
            blocks.append(jnp.sum(jnp.where(hit, term, 0.0), axis=0))
        return jnp.concatenate(blocks, axis=1)

    def back_term(stack, candidates, *held):
        g = jnp.zeros((stack.shape[1], modes, BLOCK), BF16)
        for hit, block in candidates:
            g = jnp.where(hit[:, None, None], block[None], g)
        part = jnp.einsum("hnai,nma->hnmi", stack, g, preferred_element_type=F32)
        width = part.size // owners // 8
        return scatter_sum(to_pieces(part.astype(BF16), owners, width), "subtree", *held)

    def transposed(stack, d, *held):
        part = jnp.einsum("hnij,hnmi->nmj", stack, d, preferred_element_type=F32)
        return full_sum(jnp.transpose(part, (1, 0, 2)).reshape(modes, -1), "z", *held)

    def cut(flat, target, count):
        return [(target == i, flat[:, i * BLOCK : (i + 1) * BLOCK]) for i in range(count)]

    layer = lax.axis_index("z")
    t_own = t_low - first_mid
    before, after = neighbours(stacked)
    root_received = swap(root_sent)
    before, after, root_received, t_mid, t_low, t_own, column_after, layer = (
        lax.optimization_barrier(
            (before, after, root_received, t_mid, t_low, t_own, column_after, layer)
        )
    )
    factors_root = (factor_root[0], root_received)
    window = jnp.concatenate([before, stacked, after], axis=1)
    z_part = mass_partial(window, column, mass_vals).astype(BF16)

    def of_core(flat, which):
        mid = w_root + which * w_mid
        low = w_root + 2 * w_mid + which * 2 * w_low
        return jnp.concatenate(
            [flat[:, :w_root], flat[:, mid : mid + w_mid], flat[:, low : low + 2 * w_low]], axis=1
        )

    z_part = jnp.stack([of_core(z_part, 0), of_core(z_part, 1)]).reshape(
        2, layers, modes // layers, w_root + w_own
    )
    z_part = jnp.transpose(z_part, (1, 0, 2, 3)).reshape(2 * layers, *z_part.shape[2:])
    z_part, core = lax.optimization_barrier((z_part, core))
    stacks, received = split_nodes(core, factor_low, factor_mid, update_low, update_mid)
    (z_mine,) = scatter_sum(z_part, FRONT)
    f_low, f_mid, u_low, u_mid = unpacked(stacks, received)
    (z,) = gather(z_mine.astype(BF16), "z")
    z = z.reshape(modes, -1)

    right = z[:, low_at:].reshape(modes, 2, w_low)
    y_low, t_low, t_own = forward(f_low, right, t_low, t_own)
    y, t_low, t_own = whole(y_low, (2, 2, modes, f_low.shape[-2]), t_low, t_own)
    term, t_low, t_own = update_term(u_low, y, t_low, t_own)
    acc_mid = placed(term, t_own, b_mid)
    acc_root = placed(term, t_low, b_root)
    right = (z[:, mid_at:low_at].astype(F32) - acc_mid).astype(BF16)
    right, acc_root = lax.optimization_barrier((right, acc_root))
    y_mid, t_mid = forward(f_mid, right.reshape(modes, 1, w_mid), t_mid)
    y, t_mid = whole(y_mid, (2, 1, modes, f_mid.shape[-2]), t_mid)
    term, t_mid, acc_root = update_term(u_mid, y, t_mid, acc_root)
    acc_root = acc_root + placed(term, t_mid, b_root)

    half_modes = modes // 2
    acc_root, t_mid, core = lax.optimization_barrier((acc_root, t_mid, core))

    def of_modes(value, which):
        return lax.dynamic_slice_in_dim(value, which * half_modes, half_modes, 0)

    acc_root = of_modes(acc_root, core) + swap(of_modes(acc_root, 1 - core))
    z_root = lax.dynamic_slice(z, (core * half_modes, 0), (half_modes, mid_at))
    right = (z_root.astype(F32) - acc_root).astype(BF16)

    def by_core(mine, other):
        return jnp.concatenate(
            [jnp.where(core == 0, mine, other), jnp.where(core == 0, other, mine)], axis=0
        )

    part = jnp.stack(
        [jnp.einsum("ij,mj->mi", f, right, preferred_element_type=F32) for f in factors_root]
    )
    (y_root,) = scatter_sum(to_pieces(part.astype(BF16), owners, 2 * BLOCK), "subtree")

    d_root, t_mid, core = whole(y_root, part.shape, t_mid, core)
    part = sum(
        jnp.einsum("ij,mi->mj", f, d, preferred_element_type=F32)
        for f, d in zip(factors_root, d_root)
    )
    s_half, t_mid, core = full_sum(part, "z", t_mid, core)
    s_other = swap(s_half)
    x_root = by_core(s_half.astype(BF16), s_other.astype(BF16))
    x_root = lax.optimization_barrier(x_root)
    root_blocks = cut(x_root, t_mid, b_root)
    v_mid, y_mid, x_root = back_term(u_mid, root_blocks, y_mid, x_root)
    d_mid, x_root = whole(y_mid - v_mid, (2, 1, modes, f_mid.shape[-2]), x_root)
    s_mid, x_root, t_low, t_own = transposed(f_mid, d_mid, x_root, t_low, t_own)
    x_mid = s_mid.astype(BF16)
    blocks = cut(x_root, t_low, b_root) + cut(x_mid, t_own, b_mid)
    v_low, y_low, x_mid, x_root = back_term(u_low, blocks, y_low, x_mid, x_root)
    d_low, x_mid, x_root = whole(y_low - v_low, (2, 2, modes, f_low.shape[-2]), x_mid, x_root)
    s_low, x_mid, x_root, s_half, s_other, column_after, core, layer = transposed(
        f_low, d_low, x_mid, x_root, s_half, s_other, column_after, core, layer
    )
    x_low = s_low.astype(BF16)

    y_own = jnp.concatenate([x_root, x_mid, x_low], axis=1)
    before, after = neighbours(y_own)
    own = y_own[:, w_root:]
    other = swap(own)
    first = jnp.where(core == 0, own, other)
    second = jnp.where(core == 0, other, own)
    y_all = jnp.concatenate(
        [x_root, first[:, :w_mid], second[:, :w_mid], first[:, w_mid:], second[:, w_mid:]], axis=1
    )
    before, after, other, y_all = lax.optimization_barrier((before, after, other, y_all))
    others = swap(jnp.concatenate([before[:, w_root:], after[:, w_root:]], axis=1))
    window = jnp.concatenate(
        [before, y_own, after, others[:, :w_own], other, others[:, w_own:]], axis=1
    )
    my_part = mass_partial(window, column_after, mass_vals).astype(BF16)

    mass_part = jnp.einsum("jr,kr->jk", y_all, my_part, preferred_element_type=F32)
    size = modes // layers
    y_mine = lax.dynamic_slice_in_dim(y_own, layer * size, size, axis=0)
    rows = lax.broadcasted_iota(jnp.int32, y_mine.shape, 1)
    y_mine = jnp.where((core == 0) | (rows >= w_root), y_mine, 0).astype(BF16)
    stiff_part = jnp.einsum("jr,kr->jk", y_mine, z, preferred_element_type=F32)

    def paired(value):
        size = value.shape[0] // 2
        return jnp.concatenate([value[:size], value[size:]], axis=1)

    n_mass, n_stiff = modes // 2, size // 2
    grams = jnp.concatenate([paired(mass_part), paired(stiff_part)], axis=0)
    grams = jnp.pad(grams, ((0, -(n_mass + n_stiff) % 8), (0, 0)))
    grams, y_all, s_half, s_other = full_sum(grams, "subtree", y_all, s_half, s_other)
    (grams,) = gather(grams.astype(BF16), FRONT)
    stiff, mass = unpaired(grams, n_mass, n_stiff)

    def output(flat, count):
        return jnp.transpose(flat.reshape(modes, count, -1), (1, 0, 2)).astype(F32)

    low_from = w_root + 2 * w_mid
    solved_root = by_core(s_half, s_other)[None]
    solved_mid = output(y_all[:, w_root:low_from], 2)
    solved_low = output(y_all[:, low_from:], 4)
    return solved_root, solved_mid, solved_low, stiff, mass


def solution(mesh):
    owners, fronts = mesh.shape["subtree"], mesh.shape["front"]
    split = Mesh(mesh.devices.reshape(owners, fronts // 2, 2), ("subtree", *FRONT))
    factor = P(None, FRONT, "subtree")
    update = P(None, "subtree", FRONT)
    rows = P(None, None, "subtree")

    return jax.shard_map(
        per_device,
        mesh=split,
        in_specs=(
            rows,
            rows,
            rows,
            factor,
            factor,
            factor,
            update,
            update,
            P(None, "subtree"),
            P(None, "subtree"),
            P("subtree", FRONT, None, None),
            P("subtree", FRONT),
        ),
        out_specs=(rows, rows, rows, P(), P()),
        check_vma=False,
    )
```
